256 devices in a mesh: rows: 4 (over y), half: 2 (over core), obs: 32 (over z, x).
Axes of the slice: x: 4, y: 4, z: 8, core: 2. Of those that a mesh axis runs over, the one named last changes fastest.
Arguments:
- ens_state: bfloat16 [2, 8192, 256], P('half', ('rows', 'obs')), may hold values from -6 to 6
- state_pos: bfloat16 [8192], P(('rows', 'obs')), may hold values from 0 to 1
- obs_ens: bfloat16 [2, 2, 65536, 256], P(None, 'half', ('rows', 'obs')), may hold values from -6 to 6
- obs_pos: bfloat16 [2, 65536], P(None, ('rows', 'obs')), may hold values from 0 to 1
- innov_weight: bfloat16 [2, 2, 65536, 256], P(None, 'half', ('rows', 'obs')), may hold values from -0.875 to 0.875
- block_rows: int32 [2, 512, 16], replicated, may hold values from 0 to 63, as said below
Outputs:
- increment: float32 [2, 8192, 256], P('half', ('rows', 'obs'))
The draws below stay inside these ranges and needn't reach their ends.
Inputs may be any that keep to these rules, and one draw needn't show every extreme that they name: `block_rows`: each row lists 16 different state blocks. Counting state blocks in aligned ranges of 16, an observation block names at most 8 blocks of one range, and in every aligned group of 16 observation blocks some range is named exactly 8 times by each block of the group.
All inputs are finite; a program needn't handle non-finite values.
Results may differ from the reference program's by a relative error of at most 0.0029.
Values may be sent and summed in bfloat16 or wider, within the bound.
No kernel may reach another device: no remote copies, remote signals or barrier semaphores. Data moves between devices by JAX's collectives and lax.ppermute only.
A program may use at most 64 MiB of HBM per device.

```python
import jax
import jax.numpy as jnp
from jax import lax

BLOCK = 128
MEMBERS = 256
ROW_BLOCKS = 16
OBS_BLOCKS = 16
BATCHES = 2
ALL_ROW_BLOCKS = 64
ALL_OBS_BLOCKS = 512
STATE_ROWS = 8192
OBSERVATIONS = 65536
N_ROWS = 4
N_OBS = 32


def draw_block_rows(key, part):
    half_cap = ROW_BLOCKS // 2
    block_count = OBS_BLOCKS * N_OBS
    range_count = N_ROWS
    key_busy, key_cuts, key_order = jax.random.split(key, 3)
    busy_range = jax.random.randint(key_busy, (BATCHES, N_OBS), 0, range_count)
    busy_range = jnp.repeat(busy_range, OBS_BLOCKS, axis=1)
    cut_points = jnp.sort(jax.random.randint(key_cuts, (BATCHES, block_count, 2), 0, half_cap + 1), axis=-1)
    spread = jnp.stack([cut_points[..., 0], cut_points[..., 1] - cut_points[..., 0], half_cap - cut_points[..., 1]], axis=-1)
    range_iota = jnp.arange(range_count, dtype=jnp.int32)
    is_busy = range_iota[None, None, :] == busy_range[..., None]
    other_rank = range_iota[None, None, :] - (range_iota[None, None, :] > busy_range[..., None]).astype(jnp.int32)
    other_rank = jnp.clip(other_rank, 0, 2)
    counts = jnp.where(is_busy, half_cap, jnp.take_along_axis(spread, other_rank, axis=-1))
    scores = jax.random.randint(key_order, (BATCHES, block_count, range_count, ROW_BLOCKS), 0, 1 << 20) * ROW_BLOCKS + jnp.arange(ROW_BLOCKS, dtype=jnp.int32)
    shuffled = jnp.argsort(scores, axis=-1).astype(jnp.int32)[..., :half_cap]
    candidates = range_iota[None, None, :, None] * ROW_BLOCKS + shuffled
    alive_mask = jnp.arange(half_cap, dtype=jnp.int32)[None, None, None, :] < counts[..., None]
    candidates = candidates.reshape(BATCHES, block_count, range_count * half_cap)
    alive_mask = alive_mask.reshape(BATCHES, block_count, range_count * half_cap)
    ranking = jnp.where(alive_mask, 0, 1) * (range_count * half_cap) + jnp.arange(range_count * half_cap, dtype=jnp.int32)
    selection = jnp.argsort(ranking, axis=-1)[..., :ROW_BLOCKS * N_ROWS // 4]
    return jnp.take_along_axis(candidates, selection, axis=-1).astype(jnp.int32)


def shard_levels(key, dims, shards, low, high):
    def one(dim, shards_of):
        heights = jax.random.uniform(jax.random.fold_in(jax.random.fold_in(key, 6), dim), (shards_of,), jnp.float32, low / len(shards), high / len(shards))
        return jnp.repeat(jnp.exp(heights), dims[dim] // shards_of).reshape((-1,) + (1,) * (len(dims) - dim - 1))

    gain = one(*shards[0])
    for cut in shards[1:]:
        gain = gain * one(*cut)
    return gain


def normal_values(own_key, dims, scale, limit, cuts=(), held_as=jnp.bfloat16):
    gain = shard_levels(own_key, dims, cuts, -0.22, 0.18) if cuts else 1.0
    drawn = jax.random.normal(own_key, dims, jnp.float32) * scale * gain
    return jnp.minimum(jnp.maximum(drawn, -limit), limit).astype(held_as)


def setup_inputs(seed: int = 0) -> dict:
    seeds = jax.random.split(jax.random.key(seed), 7)
    ens_state = normal_values(seeds[0], (2, STATE_ROWS, MEMBERS), 1.0, 6.0, ((0, 2), (1, 128)))
    state_pos = jnp.clip(1.0 * jax.random.uniform(seeds[1], (STATE_ROWS,), jnp.float32) ** shard_levels(seeds[1], (STATE_ROWS,), ((0, 128),), -0.2, 0.2), 0.0, 1.0).astype(jnp.bfloat16)
    obs_ens = normal_values(seeds[2], (BATCHES, 2, OBSERVATIONS, MEMBERS), 1.0, 6.0, ((1, 2), (2, 128)))
    obs_pos = jnp.clip(1.0 * jax.random.uniform(seeds[3], (BATCHES, OBSERVATIONS), jnp.float32) ** shard_levels(seeds[3], (BATCHES, OBSERVATIONS), ((1, 128),), -0.2, 0.2), 0.0, 1.0).astype(jnp.bfloat16)
    innov_weight = normal_values(seeds[4], (BATCHES, 2, OBSERVATIONS, MEMBERS), 0.15, 0.875, ((1, 2), (2, 128)))
    block_rows = draw_block_rows(jax.random.fold_in(seeds[6], 71), 0)
    return {"ens_state": ens_state, "state_pos": state_pos, "obs_ens": obs_ens, "obs_pos": obs_pos, "innov_weight": innov_weight, "block_rows": block_rows}


def reference(ens_state, state_pos, obs_ens, obs_pos, innov_weight, block_rows):
    member_count = ens_state.shape[2]
    place_tiles = state_pos.astype(jnp.float32).reshape(ALL_ROW_BLOCKS, BLOCK)
    results = []
    for target in range(2):
        source = 1 - target
        state_tiles = ens_state[source].reshape(ALL_ROW_BLOCKS, BLOCK, member_count)

        def visit(running, entries, state_tiles=state_tiles):
            obs_tile, obs_place, weight_tile, named = entries
            gathered = state_tiles[named].reshape(-1, member_count)
            positions = place_tiles[named].reshape(-1)
            products = jnp.dot(gathered, obs_tile.T, preferred_element_type=jnp.float32)
            distance = positions[:, None] - obs_place[None, :]
            damping = jnp.exp(-4.0 * distance * distance)
            scaled = (products * damping / (member_count - 1)).astype(jnp.bfloat16)
            additions = jnp.dot(scaled, weight_tile, preferred_element_type=jnp.float32)
            running = running.at[named].add(additions.reshape(-1, BLOCK, member_count))
            return running, None

        running = jnp.zeros((ALL_ROW_BLOCKS, BLOCK, member_count), jnp.float32)
        for batch_index in range(BATCHES):
            entries = (obs_ens[batch_index, source].reshape(ALL_OBS_BLOCKS, BLOCK, member_count),
                       obs_pos[batch_index].astype(jnp.float32).reshape(ALL_OBS_BLOCKS, BLOCK),
                       innov_weight[batch_index, target].reshape(ALL_OBS_BLOCKS, BLOCK, member_count),
                       block_rows[batch_index].astype(jnp.int32))
            running, _ = lax.scan(visit, running, entries)
        results.append(running.reshape(STATE_ROWS, member_count))
    return jnp.stack(results)
```

```python
import functools
import math

import jax
import jax.numpy as jnp
from jax import lax
from jax.experimental import pallas as pl
from jax.experimental.pallas import tpu as pltpu
from jax.sharding import PartitionSpec as P


BATCHES = 2
ROWS, HALVES, OBS = 4, 2, 32
NX, NZ = 4, 8
EDGE = 128
SHARD = 64
MEMBERS = 256
RANGE_BLOCKS = 16
SPAN = 4
NAMED = 16
CAP = 8
GROUP = 4
DEAD = -1e30
Z_ORDER = (0, 4, 2, 6, 1, 5, 3, 7)


def partner(value):
    return lax.ppermute(value, "half", [(0, 1), (1, 0)])


def along_rows(value, step):
    return lax.ppermute(value, "rows", [(s, (s + step) % ROWS) for s in range(ROWS)])


def along_rows_partner(value, step):
    pairs = [
        (r * HALVES + h, ((r + step) % ROWS) * HALVES + 1 - h)
        for r in range(ROWS)
        for h in range(HALVES)
    ]
    return lax.ppermute(value, ("rows", "half"), pairs)


def swap_z(value, mask):
    pairs = [(z * NX + x, (z ^ mask) * NX + x) for z in range(NZ) for x in range(NX)]
    return lax.ppermute(value, "obs", pairs)


def along_x(value, step):
    pairs = [(z * NX + x, z * NX + (x + step) % NX) for z in range(NZ) for x in range(NX)]
    return lax.ppermute(value, "obs", pairs)


def compute_kernel(
    place_ref, named_ref, s0, s1, s2, s3, oo, wo, ol, wl, orr, wr, oa, wa, ob, wb,
    out_ref, state, spot, ospot, acc, slots, counts,
):
    first = place_ref[0] * RANGE_BLOCKS
    my_z = place_ref[1] // NX
    my_x = lax.rem(place_ref[1], NX)
    for k, piece in enumerate((s0, s1, s2, s3)):
        src_x = lax.rem(my_x + (NX - k), NX)
        for p, mask in enumerate(Z_ORDER):
            src = (my_z ^ mask) * NX + src_x
            state[src] = piece[p * SHARD : (p + 1) * SHARD, :MEMBERS]
            spot[src] = piece[p * SHARD : (p + 1) * SHARD, MEMBERS:].astype(jnp.float32) * 2.0
    sources = (
        (oo, wo, 0, 0), (oo, wo, 1, 1), (ol, wl, 0, 2), (ol, wl, 1, 3),
        (orr, wr, 0, 4), (orr, wr, 1, 5), (oa, wa, 0, 6), (ob, wb, 0, 7),
    )
    rows = SPAN * EDGE
    for o, _, t, n in sources:
        ospot[n] = o[t, rows : rows + 16, :EDGE].astype(jnp.float32) * 2.0
    acc[...] = jnp.zeros_like(acc)

    def fill(n, carry):
        def put(e, count):
            relative = named_ref[n * NAMED + e] - first
            inside = jnp.logical_and(relative >= 0, relative < RANGE_BLOCKS)
            slots[n * NAMED + count] = jnp.where(inside, relative, 0)
            return count + inside.astype(jnp.int32)

        count = 0
        for e in range(NAMED):
            count = put(e, count)
        for e in range(GROUP):
            @pl.when(count + e < NAMED)
            def _():
                slots[n * NAMED + jnp.minimum(count + e, NAMED - 1)] = 0
        counts[n] = count
        return carry

    lax.fori_loop(0, 8 * SPAN, fill, 0)
    scale = math.log(1.0 / (MEMBERS - 1))

    for o, w, t, n in sources:
        def block(i, carry, o=o, w=w, t=t, n=n):
            index = n * SPAN + i
            start = pl.multiple_of(i * EDGE, EDGE)
            obs = o[t, pl.ds(start, EDGE), :]
            weight = w[t, pl.ds(start, EDGE), :]
            place = ospot[n, pl.ds(i, 1), :]
            count = counts[index]

            def group(g, inner):
                picks = [slots[index * NAMED + g * GROUP + k] for k in range(GROUP)]
                gathered = jnp.concatenate(
                    [state[pl.ds(2 * b, 2)].reshape(EDGE, MEMBERS) for b in picks], axis=0
                )
                products = lax.dot_general(
                    gathered, obs, (((1,), (1,)), ((), ())), preferred_element_type=jnp.float32
                )
                tiles = []
                for k, b in enumerate(picks):
                    shift = jnp.where(g * GROUP + k < count, scale, DEAD)
                    d = spot[pl.ds(2 * b, 2)].reshape(EDGE, EDGE) - place
                    damping = jnp.exp(shift - d * d)
                    tiles.append((products[k * EDGE : (k + 1) * EDGE] * damping).astype(jnp.bfloat16))
                added = jnp.dot(
                    jnp.concatenate(tiles, axis=0), weight, preferred_element_type=jnp.float32
                )
                for k, b in enumerate(picks):
                    acc[b] += added[k * EDGE : (k + 1) * EDGE]
                return inner

            lax.fori_loop(0, (count + GROUP - 1) // GROUP, group, 0)
            return carry

        lax.fori_loop(0, SPAN, block, 0)
    out_ref[...] = acc[...].reshape(RANGE_BLOCKS * EDGE, MEMBERS).astype(jnp.bfloat16)


def compute(place, named, arrays):
    vmem = pl.BlockSpec(memory_space=pltpu.VMEM)
    smem = pl.BlockSpec(memory_space=pltpu.SMEM)
    return pl.pallas_call(
        compute_kernel,
        out_shape=jax.ShapeDtypeStruct((RANGE_BLOCKS * EDGE, MEMBERS), jnp.bfloat16),
        in_specs=[smem, smem] + [vmem] * len(arrays),
        out_specs=vmem,
        scratch_shapes=[
            pltpu.VMEM((OBS, SHARD, MEMBERS), jnp.bfloat16),
            pltpu.VMEM((OBS, SHARD, EDGE), jnp.float32),
            pltpu.VMEM((8, 16, EDGE), jnp.float32),
            pltpu.VMEM((RANGE_BLOCKS, EDGE, MEMBERS), jnp.float32),
            pltpu.SMEM((8 * SPAN * NAMED + NAMED,), jnp.int32),
            pltpu.SMEM((8 * SPAN,), jnp.int32),
        ],
        compiler_params=pltpu.CompilerParams(vmem_limit_bytes=48 << 20),
        cost_estimate=pl.CostEstimate(
            flops=4_000_000_000, transcendentals=4_000_000, bytes_accessed=8_000_000
        ),
        name="increment",
    )(place, named, *arrays)


def local(ens_state, state_pos, obs_ens, obs_pos, innov_weight, block_rows):
    row, column = lax.axis_index("rows"), lax.axis_index("obs")
    obs_own = jnp.concatenate(
        [
            obs_ens[:, 0],
            jnp.pad(obs_pos.reshape(BATCHES, SPAN, EDGE), ((0, 0), (0, 16 - SPAN), (0, MEMBERS - EDGE))),
        ],
        axis=1,
    )
    weight = innov_weight[:, 0]
    obs_left, obs_right = along_rows(obs_own, 1), along_rows(obs_own, ROWS - 1)
    weight_left, weight_right = along_rows_partner(weight, 1), along_rows_partner(weight, ROWS - 1)
    weight_own = partner(weight)
    obs_far0, obs_far1 = along_rows(obs_left[:1], 1), along_rows(obs_right[1:], ROWS - 1)
    weight_far0, weight_far1 = along_rows(weight_left[:1], 1), along_rows(weight_right[1:], ROWS - 1)

    state = jnp.concatenate(
        [ens_state[0], jnp.broadcast_to(state_pos[:, None], (SHARD, EDGE))], axis=1
    )
    for mask in (4, 2, 1):
        state = jnp.concatenate([state, swap_z(state, mask)], axis=0)
    pieces = [state] + [along_x(state, k) for k in range(1, NX)]

    tables = block_rows.reshape(BATCHES, ROWS, OBS, SPAN, NAMED)
    tables = lax.dynamic_index_in_dim(tables, column, axis=2, keepdims=False)
    tables = jnp.stack(
        [
            lax.dynamic_index_in_dim(tables, lax.rem(row + k, ROWS), axis=1, keepdims=False)
            for k in (0, ROWS - 1, 1, 2)
        ]
    )
    arrays = (
        *pieces, obs_own, weight_own, obs_left, weight_left, obs_right, weight_right,
        obs_far0, weight_far0, obs_far1, weight_far1,
    )
    partial = compute(jnp.stack([row, column]), tables.reshape(-1), arrays)
    shares = lax.all_to_all(partial, "obs", 0, 0, tiled=True)
    summed = jnp.sum(shares.reshape(OBS, SHARD, MEMBERS).astype(jnp.float32), axis=0)
    return partner(summed)[None]


def solution(mesh):
    in_specs = (
        P("half", ("rows", "obs"), None),
        P(("rows", "obs")),
        P(None, "half", ("rows", "obs"), None),
        P(None, ("rows", "obs")),
        P(None, "half", ("rows", "obs"), None),
        P(),
    )
    out_specs = P("half", ("rows", "obs"), None)
    return jax.shard_map(local, mesh=mesh, in_specs=in_specs, out_specs=out_specs, check_vma=False)
```

```python
import math

import jax
import jax.numpy as jnp
from jax import lax
from jax.experimental import pallas as pl
from jax.experimental.pallas import tpu as pltpu
from jax.sharding import PartitionSpec as P


BATCHES = 2
ROWS, HALVES, OBS = 4, 2, 32
NX, NZ = 4, 8
EDGE = 128
SHARD = 64
MEMBERS = 256
RANGE_BLOCKS = 16
SPAN = 4
NAMED = 16
OBS_ROWS = SPAN * EDGE
PAD = 16
Z_ORDER = (0, 4, 2, 6, 1, 5, 3, 7)

GROUP = 8
SOURCES = ((0, 2, 0), (3, 2, 0), (1, 2, 0), (2, 1, 0), (2, 1, 1))
PICKS = 8 * NAMED + GROUP
VISITS = 8 * NAMED // GROUP
DEAD = -1e30
LIVE = math.log2(1.0 / (MEMBERS - 1))
STRETCH = 2.0 * math.sqrt(math.log2(math.e))

VMEM = pl.BlockSpec(memory_space=pltpu.VMEM)
SMEM = pl.BlockSpec(memory_space=pltpu.SMEM)


def flip(value):
    return lax.ppermute(value, "half", [(0, 1), (1, 0)])


def along_rows(value, step):
    return lax.ppermute(value, "rows", [(s, (s + step) % ROWS) for s in range(ROWS)])


def along_rows_flip(value, step):
    pairs = [
        (r * HALVES + h, ((r + step) % ROWS) * HALVES + 1 - h)
        for r in range(ROWS)
        for h in range(HALVES)
    ]
    return lax.ppermute(value, ("rows", "half"), pairs)


def swap_z(value, mask):
    pairs = [(z * NX + x, (z ^ mask) * NX + x) for z in range(NZ) for x in range(NX)]
    return lax.ppermute(value, "obs", pairs)


def swap_z_flip(value, mask):
    pairs = [
        (h * OBS + z * NX + x, (1 - h) * OBS + (z ^ mask) * NX + x)
        for h in range(HALVES)
        for z in range(NZ)
        for x in range(NX)
    ]
    return lax.ppermute(value, ("half", "obs"), pairs)


def along_x(value, step):
    pairs = [(z * NX + x, z * NX + (x + step) % NX) for z in range(NZ) for x in range(NX)]
    return lax.ppermute(value, "obs", pairs)


def lists_kernel(place_ref, named_ref, picks, shifts, blocks, totals):
    row, column = place_ref[0], place_ref[1]
    first = row * RANGE_BLOCKS
    for s, (turn, batches, batch) in enumerate(SOURCES):
        owner = jnp.bitwise_and(row + turn, ROWS - 1) * OBS + column

        def fill(i, visits, s=s, batch=batch, owner=owner):
            t = batch + lax.shift_right_logical(i, 2)
            place = owner * SPAN + jnp.bitwise_and(i, SPAN - 1)
            base = s * PICKS + visits * GROUP
            count = jnp.int32(0)
            for e in range(NAMED):
                relative = named_ref[t, e, place] - first
                inside = jnp.logical_and(relative >= 0, relative < RANGE_BLOCKS)
                picks[base + count] = jnp.where(inside, relative, 0)
                shifts[base + count] = LIVE
                count = count + inside.astype(jnp.int32)
            for e in range(GROUP - 1):
                picks[base + count + e] = 0
                shifts[base + count + e] = DEAD
            more = lax.shift_right_logical(count + GROUP - 1, GROUP.bit_length() - 1)
            for k in range(NAMED // GROUP):

                @pl.when(k < more)
                def _(k=k):
                    blocks[s * VISITS + visits + k] = i

            return visits + more

        totals[s] = lax.fori_loop(0, batches * SPAN, fill, jnp.int32(0))


def make_lists(place, named):
    return pl.pallas_call(
        lists_kernel,
        out_shape=(
            jax.ShapeDtypeStruct((len(SOURCES) * PICKS,), jnp.int32),
            jax.ShapeDtypeStruct((len(SOURCES) * PICKS,), jnp.float32),
            jax.ShapeDtypeStruct((len(SOURCES) * VISITS,), jnp.int32),
            jax.ShapeDtypeStruct((8,), jnp.int32),
        ),
        in_specs=[SMEM, SMEM],
        out_specs=(SMEM,) * 4,
        cost_estimate=pl.CostEstimate(flops=4_000_000, transcendentals=0, bytes_accessed=4_000_000),
        name="lists",
    )(place, named)


def visit(s, obs, weights, places, state, spot, acc, tiles, picks, shifts, blocks, totals):
    total = totals[s]

    def make_tiles(g):
        i = blocks[s * VISITS + g]
        t, r = lax.shift_right_logical(i, 2), jnp.bitwise_and(i, SPAN - 1)
        here = obs[t, pl.ds(pl.multiple_of(r * EDGE, EDGE), EDGE), :]
        place = places[pl.ds(i, 1), :]
        chosen = [picks[s * PICKS + g * GROUP + k] for k in range(GROUP)]
        gathered = jnp.concatenate(
            [state[pl.ds(2 * b, 2)].reshape(EDGE, MEMBERS) for b in chosen], axis=0
        )
        products = lax.dot_general(
            gathered, here, (((1,), (1,)), ((), ())), preferred_element_type=jnp.float32
        )
        for k, b in enumerate(chosen):
            shift = shifts[s * PICKS + g * GROUP + k]
            d = spot[pl.ds(2 * b, 2)].reshape(EDGE, EDGE) - place
            damped = products[k * EDGE : (k + 1) * EDGE] * jnp.exp2(shift - d * d)
            tiles[k * EDGE : (k + 1) * EDGE] = damped.astype(jnp.bfloat16)

    def add_tiles(g):
        i = blocks[s * VISITS + g]
        weight = weights[pl.ds(pl.multiple_of(i * EDGE, EDGE), EDGE), :]
        chosen = [picks[s * PICKS + g * GROUP + k] for k in range(GROUP)]
        added = jnp.dot(tiles[...], weight, preferred_element_type=jnp.float32)
        for k, b in enumerate(chosen):
            acc[b] += added[k * EDGE : (k + 1) * EDGE]

    @pl.when(total > 0)
    def _():
        make_tiles(0)

        def step(g, carry):
            add_tiles(g - 1)
            make_tiles(g)
            return carry

        lax.fori_loop(1, total, step, 0)
        add_tiles(total - 1)


def read_places(obs, places):
    for t in range(obs.shape[0]):
        rows = obs[t, OBS_ROWS : OBS_ROWS + PAD, :EDGE].astype(jnp.float32)
        places[t * SPAN : (t + 1) * SPAN] = rows[:SPAN] * STRETCH


def near_kernel(
    place_ref, picks, shifts, blocks, totals, s0, s1, s2, s3, oo, wo, ol, wl, orr, wr,
    state, spot, acc, places, tiles,
):
    my_z = lax.shift_right_logical(place_ref[1], 2)
    my_x = jnp.bitwise_and(place_ref[1], NX - 1)
    lanes = lax.broadcasted_iota(jnp.int32, (SHARD, EDGE), 1)
    sublanes = lax.broadcasted_iota(jnp.int32, (SHARD, EDGE), 0)
    same = lanes == sublanes
    ones = jnp.ones((EDGE, EDGE), jnp.bfloat16)
    for k, piece in enumerate((s0, s1, s2, s3)):
        src_x = jnp.bitwise_and(my_x + (NX - k), NX - 1)
        held = piece[NZ * SHARD : NZ * SHARD + PAD, :EDGE].astype(jnp.float32)
        spread = jnp.concatenate(
            [jnp.where(same, held[p : p + 1], 0.0) for p in range(NZ)], axis=0
        ).astype(jnp.bfloat16)
        columns = jnp.dot(spread, ones, preferred_element_type=jnp.float32) * STRETCH
        for p, mask in enumerate(Z_ORDER):
            src = (my_z ^ mask) * NX + src_x
            state[src] = piece[p * SHARD : (p + 1) * SHARD, :]
            spot[src] = columns[p * SHARD : (p + 1) * SHARD]
    acc[...] = jnp.zeros_like(acc)
    for s, (o, w) in enumerate(((oo, wo), (ol, wl), (orr, wr))):
        read_places(o, places)
        w = w.reshape(BATCHES * OBS_ROWS, MEMBERS)
        visit(s, o, w, places, state, spot, acc, tiles, picks, shifts, blocks, totals)


def near(place, lists, arrays):
    return pl.pallas_call(
        near_kernel,
        out_shape=(
            jax.ShapeDtypeStruct((OBS, SHARD, MEMBERS), jnp.bfloat16),
            jax.ShapeDtypeStruct((OBS, SHARD, EDGE), jnp.float32),
            jax.ShapeDtypeStruct((RANGE_BLOCKS, EDGE, MEMBERS), jnp.float32),
        ),
        in_specs=[SMEM] * 5 + [VMEM] * 10,
        out_specs=(VMEM,) * 3,
        scratch_shapes=[
            pltpu.VMEM((8, EDGE), jnp.float32),
            pltpu.VMEM((GROUP * EDGE, EDGE), jnp.bfloat16),
        ],
        compiler_params=pltpu.CompilerParams(vmem_limit_bytes=24 << 20),
        cost_estimate=pl.CostEstimate(
            flops=4_000_000_000, transcendentals=4_000_000, bytes_accessed=8_000_000
        ),
        name="near",
    )(place, *lists, *arrays)


def far_kernel(
    picks, shifts, blocks, totals, state, spot, near_acc, oa, wa, ob, wb, out,
    places, tiles, acc,
):
    acc[...] = near_acc[...]
    for s, (o, w) in ((3, (oa, wa)), (4, (ob, wb))):
        read_places(o, places)
        w = w.reshape(OBS_ROWS, MEMBERS)
        visit(s, o, w, places, state, spot, acc, tiles, picks, shifts, blocks, totals)
    out[...] = acc[...].reshape(RANGE_BLOCKS * EDGE, MEMBERS).astype(jnp.bfloat16)


def far(lists, state, spot, acc, arrays):
    return pl.pallas_call(
        far_kernel,
        out_shape=jax.ShapeDtypeStruct((RANGE_BLOCKS * EDGE, MEMBERS), jnp.bfloat16),
        in_specs=[SMEM] * 4 + [VMEM] * 7,
        out_specs=VMEM,
        scratch_shapes=[
            pltpu.VMEM((8, EDGE), jnp.float32),
            pltpu.VMEM((GROUP * EDGE, EDGE), jnp.bfloat16),
            pltpu.VMEM((RANGE_BLOCKS, EDGE, MEMBERS), jnp.float32),
        ],
        compiler_params=pltpu.CompilerParams(vmem_limit_bytes=24 << 20),
        cost_estimate=pl.CostEstimate(
            flops=1_000_000_000, transcendentals=1_000_000, bytes_accessed=8_000_000
        ),
        name="far",
    )(*lists, state, spot, acc, *arrays)


def pack_kernel(a, b, out):
    held = SHARD + PAD
    places = []
    for p in range(NZ):
        ref, q = (a, p) if p < NZ // 2 else (b, p - NZ // 2)
        out[p * SHARD : (p + 1) * SHARD] = ref[q * held : q * held + SHARD]
        places.append(ref[q * held + SHARD : (q + 1) * held].astype(jnp.float32)[:1])
    places.append(jnp.zeros((PAD - NZ, MEMBERS), jnp.float32))
    out[NZ * SHARD :] = jnp.concatenate(places, axis=0).astype(jnp.bfloat16)


def pack(a, b):
    return pl.pallas_call(
        pack_kernel,
        out_shape=jax.ShapeDtypeStruct((NZ * SHARD + PAD, MEMBERS), jnp.bfloat16),
        in_specs=[VMEM, VMEM],
        out_specs=VMEM,
        compiler_params=pltpu.CompilerParams(vmem_limit_bytes=4 << 20),
        name="pack",
    )(a, b)


def join_kernel(*refs):
    out = refs[-1]
    start = 0
    for ref in refs[:-1]:
        out[start : start + ref.shape[0]] = ref[...]
        start += ref.shape[0]


def join(*parts):
    rows = sum(part.shape[0] for part in parts)
    return pl.pallas_call(
        join_kernel,
        out_shape=jax.ShapeDtypeStruct((rows, MEMBERS), jnp.bfloat16),
        in_specs=[VMEM] * len(parts),
        out_specs=VMEM,
        compiler_params=pltpu.CompilerParams(vmem_limit_bytes=4 << 20),
        name="join",
    )(*parts)


def local(ens_state, state_pos, obs_ens, obs_pos, innov_weight, block_rows):
    place = jnp.stack([lax.axis_index("rows"), lax.axis_index("obs")])
    state = jnp.concatenate(
        [ens_state[0], jnp.pad(state_pos[None, :], ((0, PAD - 1), (0, MEMBERS - SHARD)))], axis=0
    )
    mine = flip(state)
    other = swap_z_flip(state, 4)
    state = join(mine, other)
    other = swap_z(state, 2)
    state = join(state, other)
    other = swap_z(state, 1)
    state = pack(state, other)
    pieces = [state]
    for k in range(1, NX):
        pieces.append(along_x(state, k))

    weight = innov_weight[:, 0]
    weight_left = along_rows(weight, 1)
    weight_right = along_rows(weight, ROWS - 1)
    obs = jnp.concatenate(
        [
            obs_ens[:, 0],
            jnp.pad(
                obs_pos.reshape(BATCHES, SPAN, EDGE),
                ((0, 0), (0, PAD - SPAN), (0, MEMBERS - EDGE)),
            ),
        ],
        axis=1,
    )
    obs_left = along_rows_flip(obs, 1)
    obs_right = along_rows_flip(obs, ROWS - 1)
    obs_own = flip(obs)
    weight_far0 = along_rows(weight_left[:1], 1)
    weight_far1 = along_rows(weight_right[1:], ROWS - 1)
    obs_far0 = along_rows(obs_left[:1], 1)
    obs_far1 = along_rows(obs_right[1:], ROWS - 1)

    lists = make_lists(place, jnp.transpose(block_rows, (0, 2, 1)))
    held = near(
        place,
        lists,
        (*pieces, obs_own, weight, obs_left, weight_left, obs_right, weight_right),
    )
    partial = far(lists, *held, (obs_far0, weight_far0, obs_far1, weight_far1))
    shares = lax.all_to_all(partial, "obs", 0, 0, tiled=True)
    shares = shares.reshape(OBS, SHARD, MEMBERS).astype(jnp.float32)
    return jnp.sum(shares, axis=0)[None]


def solution(mesh):
    in_specs = (
        P("half", ("rows", "obs"), None),
        P(("rows", "obs")),
        P(None, "half", ("rows", "obs"), None),
        P(None, ("rows", "obs")),
        P(None, "half", ("rows", "obs"), None),
        P(),
    )
    out_specs = P("half", ("rows", "obs"), None)
    return jax.shard_map(local, mesh=mesh, in_specs=in_specs, out_specs=out_specs, check_vma=False)
```

```python
import functools
import math

import jax
import jax.numpy as jnp
from jax import lax
from jax.experimental import pallas as pl
from jax.experimental.pallas import tpu as pltpu
from jax.sharding import PartitionSpec as P


BATCHES = 2
ROWS, HALVES, OBS = 4, 2, 32
NX, NZ = 4, 8
EDGE = 128
SHARD = 64
MEMBERS = 256
RANGE_BLOCKS = 16
SPAN = 4
NAMED = 16
OBS_ROWS = SPAN * EDGE
PAD = 16
Z_ORDER = (0, 4, 2, 6, 1, 5, 3, 7)

GROUP = 8
SOURCES = ((0, 2, 0), (3, 2, 0), (1, 2, 0), (2, 1, 0), (2, 1, 1))
PICKS = 8 * GROUP + NAMED
VISITS = 8
BLOCKS = len(SOURCES) * PICKS
TOTALS = BLOCKS + len(SOURCES) * VISITS + 8
LIVE = math.log2(1.0 / (MEMBERS - 1))
STRETCH = 2.0 * math.sqrt(math.log2(math.e))

VMEM = pl.BlockSpec(memory_space=pltpu.VMEM)
SMEM = pl.BlockSpec(memory_space=pltpu.SMEM)


def flip(value):
    return lax.ppermute(value, "half", [(0, 1), (1, 0)])


def along_rows(value, step):
    return lax.ppermute(value, "rows", [(s, (s + step) % ROWS) for s in range(ROWS)])


def along_rows_flip(value, step):
    pairs = [
        (r * HALVES + h, ((r + step) % ROWS) * HALVES + 1 - h)
        for r in range(ROWS)
        for h in range(HALVES)
    ]
    return lax.ppermute(value, ("rows", "half"), pairs)


def swap_z(value, mask):
    pairs = [(z * NX + x, (z ^ mask) * NX + x) for z in range(NZ) for x in range(NX)]
    return lax.ppermute(value, "obs", pairs)


def swap_z_flip(value, mask):
    pairs = [
        (h * OBS + z * NX + x, (1 - h) * OBS + (z ^ mask) * NX + x)
        for h in range(HALVES)
        for z in range(NZ)
        for x in range(NX)
    ]
    return lax.ppermute(value, ("half", "obs"), pairs)


def along_x(value, step):
    pairs = [(z * NX + x, z * NX + (x + step) % NX) for z in range(NZ) for x in range(NX)]
    return lax.ppermute(value, "obs", pairs)


def lists_kernel(named_ref, lists):
    row, column = lax.axis_index("rows"), lax.axis_index("obs")
    first = row * RANGE_BLOCKS
    for s, (turn, batches, batch) in enumerate(SOURCES):
        owner = jnp.bitwise_and(row + turn, ROWS - 1) * OBS + column

        def fill(i, visits, s=s, batch=batch, owner=owner):
            t = batch + lax.shift_right_logical(i, 2)
            place = owner * SPAN + jnp.bitwise_and(i, SPAN - 1)
            start = s * PICKS + visits * GROUP
            for k in range(GROUP):
                lists[start + k] = RANGE_BLOCKS
            write = start
            for e in range(NAMED):
                relative = named_ref[t, e, place] - first
                inside = jnp.bitwise_and(relative, -RANGE_BLOCKS) == 0
                lists[write] = jnp.where(inside, relative, RANGE_BLOCKS)
                write = write + inside.astype(jnp.int32)
            lists[BLOCKS + s * VISITS + visits] = i
            return visits + (write > start).astype(jnp.int32)

        lists[TOTALS + s] = lax.fori_loop(0, batches * SPAN, fill, jnp.int32(0))


def make_lists(named):
    return pl.pallas_call(
        lists_kernel,
        out_shape=jax.ShapeDtypeStruct((TOTALS + 8,), jnp.int32),
        in_specs=[SMEM],
        out_specs=SMEM,
        compiler_params=pltpu.CompilerParams(vmem_limit_bytes=1 << 20),
        cost_estimate=pl.CostEstimate(flops=4_000_000, transcendentals=0, bytes_accessed=4_000_000),
        name="lists",
    )(named)


def visit(s, obs, weights, places, state, spot, acc, tiles, lists):
    total = lists[TOTALS + s]

    def make_tiles(g):
        i = lists[BLOCKS + s * VISITS + g]
        here = obs(i)
        place = places[pl.ds(i, 1), :]
        chosen = [lists[s * PICKS + g * GROUP + k] for k in range(GROUP)]
        gathered = jnp.concatenate(
            [state[pl.ds(2 * b, 2)].reshape(EDGE, MEMBERS) for b in chosen], axis=0
        )
        products = lax.dot_general(
            gathered, here, (((1,), (1,)), ((), ())), preferred_element_type=jnp.float32
        )
        for k, b in enumerate(chosen):
            d = spot[pl.ds(2 * b, 2)].reshape(EDGE, EDGE) - place
            damped = products[k * EDGE : (k + 1) * EDGE] * jnp.exp2(LIVE - d * d)
            tiles[k * EDGE : (k + 1) * EDGE] = damped.astype(jnp.bfloat16)

    def add_tiles(g):
        weight = weights(lists[BLOCKS + s * VISITS + g])
        chosen = [lists[s * PICKS + g * GROUP + k] for k in range(GROUP)]
        added = jnp.dot(tiles[...], weight, preferred_element_type=jnp.float32)
        for k, b in enumerate(chosen):
            acc[b] += added[k * EDGE : (k + 1) * EDGE]

    @pl.when(total > 0)
    def _():
        make_tiles(0)

        def step(g, carry):
            add_tiles(g - 1)
            make_tiles(g)
            return carry

        lax.fori_loop(1, total, step, 0)
        add_tiles(total - 1)


def split(ref):
    def part(i):
        t, r = lax.shift_right_logical(i, 2), jnp.bitwise_and(i, SPAN - 1)
        return ref[t, pl.ds(pl.multiple_of(r * EDGE, EDGE), EDGE), :]

    return part


def flat(ref, start):
    def part(i):
        return ref[pl.ds(pl.multiple_of(start + i * EDGE, PAD), EDGE), :]

    return part


def spread_places(held, places, start):
    places[start : start + SPAN] = held.astype(jnp.float32)[:SPAN] * STRETCH


def near_kernel(
    lists, s0, s1, s2, s3, oo, wo, ol, wl, orr, wr, state, spot, acc, places, tiles,
):
    column = lax.axis_index("obs")
    my_z = lax.shift_right_logical(column, 2)
    my_x = jnp.bitwise_and(column, NX - 1)
    lanes = lax.broadcasted_iota(jnp.int32, (SHARD, EDGE), 1)
    sublanes = lax.broadcasted_iota(jnp.int32, (SHARD, EDGE), 0)
    same = lanes == sublanes
    ones = jnp.ones((EDGE, EDGE), jnp.bfloat16)
    for k, piece in enumerate((s0, s1, s2, s3)):
        src_x = jnp.bitwise_and(my_x + (NX - k), NX - 1)
        held = piece[NZ * SHARD : NZ * SHARD + PAD, :EDGE].astype(jnp.float32)
        spread = jnp.concatenate(
            [jnp.where(same, held[p : p + 1], 0.0) for p in range(NZ)], axis=0
        ).astype(jnp.bfloat16)
        columns = jnp.dot(spread, ones, preferred_element_type=jnp.float32) * STRETCH
        for p, mask in enumerate(Z_ORDER):
            src = (my_z ^ mask) * NX + src_x
            state[src] = piece[p * SHARD : (p + 1) * SHARD, :]
            spot[src] = columns[p * SHARD : (p + 1) * SHARD]
    state[OBS:] = jnp.zeros((2, SHARD, MEMBERS), jnp.bfloat16)
    spot[OBS:] = jnp.zeros((2, SHARD, EDGE), jnp.float32)
    acc[...] = jnp.zeros_like(acc)
    for s, (o, w) in enumerate(((oo, wo), (ol, wl), (orr, wr))):
        for t in range(BATCHES):
            spread_places(o[t, OBS_ROWS : OBS_ROWS + PAD, :EDGE], places, t * SPAN)
        visit(s, split(o), split(w), places, state, spot, acc, tiles, lists)


def near(lists, arrays):
    return pl.pallas_call(
        near_kernel,
        out_shape=(
            jax.ShapeDtypeStruct((OBS + 2, SHARD, MEMBERS), jnp.bfloat16),
            jax.ShapeDtypeStruct((OBS + 2, SHARD, EDGE), jnp.float32),
            jax.ShapeDtypeStruct((RANGE_BLOCKS + 1, EDGE, MEMBERS), jnp.float32),
        ),
        in_specs=[SMEM] + [VMEM] * 10,
        out_specs=(VMEM,) * 3,
        scratch_shapes=[
            pltpu.VMEM((8, EDGE), jnp.float32),
            pltpu.VMEM((GROUP * EDGE, EDGE), jnp.bfloat16),
        ],
        compiler_params=pltpu.CompilerParams(vmem_limit_bytes=24 << 20),
        cost_estimate=pl.CostEstimate(
            flops=4_000_000_000, transcendentals=4_000_000, bytes_accessed=8_000_000
        ),
        name="near",
    )(lists, *arrays)


def far_kernel(lists, state, spot, near_acc, left, right, out, places, tiles, acc):
    acc[...] = near_acc[...]
    for s, both in ((3, left), (4, right)):
        spread_places(both[OBS_ROWS : OBS_ROWS + PAD, :EDGE], places, 0)
        visit(
            s, flat(both, 0), flat(both, OBS_ROWS + PAD), places, state, spot, acc, tiles, lists
        )
    out[...] = acc[:RANGE_BLOCKS].reshape(RANGE_BLOCKS * EDGE, MEMBERS).astype(jnp.bfloat16)


def far(lists, state, spot, acc, arrays):
    return pl.pallas_call(
        far_kernel,
        out_shape=jax.ShapeDtypeStruct((RANGE_BLOCKS * EDGE, MEMBERS), jnp.bfloat16),
        in_specs=[SMEM] + [VMEM] * 5,
        out_specs=VMEM,
        scratch_shapes=[
            pltpu.VMEM((8, EDGE), jnp.float32),
            pltpu.VMEM((GROUP * EDGE, EDGE), jnp.bfloat16),
            pltpu.VMEM((RANGE_BLOCKS + 1, EDGE, MEMBERS), jnp.float32),
        ],
        compiler_params=pltpu.CompilerParams(vmem_limit_bytes=24 << 20),
        cost_estimate=pl.CostEstimate(
            flops=1_000_000_000, transcendentals=1_000_000, bytes_accessed=8_000_000
        ),
        name="far",
    )(lists, state, spot, acc, *arrays)


def pack_kernel(a, b, out):
    held = SHARD + PAD
    places = []
    for p in range(NZ):
        ref, q = (a, p) if p < NZ // 2 else (b, p - NZ // 2)
        out[p * SHARD : (p + 1) * SHARD] = ref[q * held : q * held + SHARD]
        places.append(ref[q * held + SHARD : (q + 1) * held].astype(jnp.float32)[:1])
    places.append(jnp.zeros((PAD - NZ, MEMBERS), jnp.float32))
    out[NZ * SHARD :] = jnp.concatenate(places, axis=0).astype(jnp.bfloat16)


def pack(a, b):
    return pl.pallas_call(
        pack_kernel,
        out_shape=jax.ShapeDtypeStruct((NZ * SHARD + PAD, MEMBERS), jnp.bfloat16),
        in_specs=[VMEM, VMEM],
        out_specs=VMEM,
        compiler_params=pltpu.CompilerParams(vmem_limit_bytes=4 << 20),
        name="pack",
    )(a, b)


def join_kernel(*refs):
    out = refs[-1]
    start = 0
    for ref in refs[:-1]:
        out[start : start + ref.shape[0]] = ref[...]
        start += ref.shape[0]


def join(*parts):
    rows = sum(part.shape[0] for part in parts)
    return pl.pallas_call(
        join_kernel,
        out_shape=jax.ShapeDtypeStruct((rows, MEMBERS), jnp.bfloat16),
        in_specs=[VMEM] * len(parts),
        out_specs=VMEM,
        compiler_params=pltpu.CompilerParams(vmem_limit_bytes=4 << 20),
        name="join",
    )(*parts)


def load_kernel(obs, places, out):
    for t in range(BATCHES):
        out[t, :OBS_ROWS] = obs[t]
        held = places[t : t + 1].astype(jnp.float32)
        rows = [held[:, r * EDGE : (r + 1) * EDGE] for r in range(SPAN)]
        rows.append(jnp.zeros((PAD - SPAN, EDGE), jnp.float32))
        out[t, OBS_ROWS:, :EDGE] = jnp.concatenate(rows, axis=0).astype(jnp.bfloat16)
        out[t, OBS_ROWS:, EDGE:] = jnp.zeros((PAD, MEMBERS - EDGE), jnp.bfloat16)


def load(obs, places):
    return pl.pallas_call(
        load_kernel,
        out_shape=jax.ShapeDtypeStruct((BATCHES, OBS_ROWS + PAD, MEMBERS), jnp.bfloat16),
        in_specs=[VMEM, VMEM],
        out_specs=VMEM,
        compiler_params=pltpu.CompilerParams(vmem_limit_bytes=8 << 20),
        name="load",
    )(obs, places)


def relay_kernel(batch, obs, weights, out):
    out[: OBS_ROWS + PAD] = obs[batch]
    out[OBS_ROWS + PAD :] = weights[batch]


def relay(batch, obs, weights):
    return pl.pallas_call(
        functools.partial(relay_kernel, batch),
        out_shape=jax.ShapeDtypeStruct((2 * OBS_ROWS + PAD, MEMBERS), jnp.bfloat16),
        in_specs=[VMEM, VMEM],
        out_specs=VMEM,
        compiler_params=pltpu.CompilerParams(vmem_limit_bytes=8 << 20),
        name="relay",
    )(obs, weights)


def local(ens_state, state_pos, obs_ens, obs_pos, innov_weight, block_rows):
    state = jnp.concatenate(
        [ens_state[0], jnp.pad(state_pos[None, :], ((0, PAD - 1), (0, MEMBERS - SHARD)))], axis=0
    )
    mine = flip(state)
    other = swap_z_flip(state, 4)
    state = join(mine, other)
    other = swap_z(state, 2)
    state = join(state, other)
    other = swap_z(state, 1)
    state = pack(state, other)
    pieces = [state]
    for k in range(1, NX):
        pieces.append(along_x(state, k))

    weight = innov_weight[:, 0]
    weight_left = along_rows(weight, 1)
    weight_right = along_rows(weight, ROWS - 1)
    obs = load(obs_ens[:, 0], obs_pos)
    obs_left = along_rows_flip(obs, 1)
    obs_right = along_rows_flip(obs, ROWS - 1)
    obs_own = flip(obs)
    far0 = relay(0, obs_left, weight_left)
    far0 = along_rows(far0, 1)
    far1 = relay(1, obs_right, weight_right)
    far1 = along_rows(far1, ROWS - 1)

    lists = make_lists(jnp.transpose(block_rows, (0, 2, 1)))
    held = near(lists, (*pieces, obs_own, weight, obs_left, weight_left, obs_right, weight_right))
    partial = far(lists, *held, (far0, far1))
    shares = lax.all_to_all(partial, "obs", 0, 0, tiled=True)
    shares = shares.reshape(OBS, SHARD, MEMBERS).astype(jnp.float32)
    return jnp.sum(shares, axis=0)[None]


def solution(mesh):
    in_specs = (
        P("half", ("rows", "obs"), None),
        P(("rows", "obs")),
        P(None, "half", ("rows", "obs"), None),
        P(None, ("rows", "obs")),
        P(None, "half", ("rows", "obs"), None),
        P(),
    )
    out_specs = P("half", ("rows", "obs"), None)
    return jax.shard_map(local, mesh=mesh, in_specs=in_specs, out_specs=out_specs, check_vma=False)
```

```python
import functools
import math

import jax
import jax.numpy as jnp
from jax import lax
from jax.experimental import pallas as pl
from jax.experimental.pallas import tpu as pltpu
from jax.sharding import PartitionSpec as P


BATCHES = 2
ROWS, HALVES, OBS = 4, 2, 32
NX, NZ = 4, 8
EDGE = 128
SHARD = 64
MEMBERS = 256
RANGE_BLOCKS = 16
SPAN = 4
NAMED = 16
OBS_ROWS = SPAN * EDGE
PAD = 16
Z_ORDER = (0, 4, 2, 6, 1, 5, 3, 7)

GROUP = 8
SOURCES = ((0, 2, 0), (3, 2, 0), (1, 2, 0), (2, 1, 0), (2, 1, 1))
PICKS = 8 * GROUP + NAMED
VISITS = 8
BLOCKS = len(SOURCES) * PICKS
TOTALS = BLOCKS + len(SOURCES) * VISITS + 8
LIVE = math.log2(1.0 / (MEMBERS - 1))
STRETCH = 2.0 * math.sqrt(math.log2(math.e))

VMEM = pl.BlockSpec(memory_space=pltpu.VMEM)
SMEM = pl.BlockSpec(memory_space=pltpu.SMEM)


def flip(value):
    return lax.ppermute(value, "half", [(0, 1), (1, 0)])


def along_rows(value, step):
    return lax.ppermute(value, "rows", [(s, (s + step) % ROWS) for s in range(ROWS)])


def along_rows_flip(value, step):
    pairs = [
        (r * HALVES + h, ((r + step) % ROWS) * HALVES + 1 - h)
        for r in range(ROWS)
        for h in range(HALVES)
    ]
    return lax.ppermute(value, ("rows", "half"), pairs)


def swap_z(value, mask):
    pairs = [(z * NX + x, (z ^ mask) * NX + x) for z in range(NZ) for x in range(NX)]
    return lax.ppermute(value, "obs", pairs)


def swap_z_flip(value, mask):
    pairs = [
        (h * OBS + z * NX + x, (1 - h) * OBS + (z ^ mask) * NX + x)
        for h in range(HALVES)
        for z in range(NZ)
        for x in range(NX)
    ]
    return lax.ppermute(value, ("half", "obs"), pairs)


def along_x(value, step):
    pairs = [(z * NX + x, z * NX + (x + step) % NX) for z in range(NZ) for x in range(NX)]
    return lax.ppermute(value, "obs", pairs)


def lists_kernel(named_ref, lists):
    row, column = lax.axis_index("rows"), lax.axis_index("obs")
    first = row * RANGE_BLOCKS
    for s, (turn, batches, batch) in enumerate(SOURCES):
        owner = jnp.bitwise_and(row + turn, ROWS - 1) * OBS + column

        def fill(i, visits, s=s, batch=batch, owner=owner):
            t = batch + lax.shift_right_logical(i, 2)
            place = owner * SPAN + jnp.bitwise_and(i, SPAN - 1)
            start = s * PICKS + visits * GROUP
            for k in range(GROUP):
                lists[start + k] = RANGE_BLOCKS
            write = start
            for e in range(NAMED):
                relative = named_ref[t, e, place] - first
                inside = jnp.bitwise_and(relative, -RANGE_BLOCKS) == 0
                lists[write] = jnp.where(inside, relative, RANGE_BLOCKS)
                write = write + inside.astype(jnp.int32)
            lists[BLOCKS + s * VISITS + visits] = i
            return visits + (write > start).astype(jnp.int32)

        lists[TOTALS + s] = lax.fori_loop(0, batches * SPAN, fill, jnp.int32(0))


def make_lists(named):
    return pl.pallas_call(
        lists_kernel,
        out_shape=jax.ShapeDtypeStruct((TOTALS + 8,), jnp.int32),
        in_specs=[SMEM],
        out_specs=SMEM,
        compiler_params=pltpu.CompilerParams(vmem_limit_bytes=1 << 20),
        cost_estimate=pl.CostEstimate(flops=4_000_000, transcendentals=0, bytes_accessed=4_000_000),
        name="lists",
    )(named)


def visit(s, obs, weights, places, state, spot, acc, tiles, lists):
    total = lists[TOTALS + s]

    def make_tiles(g):
        i = lists[BLOCKS + s * VISITS + g]
        here = obs(i)
        place = places[pl.ds(i, 1), :]
        chosen = [lists[s * PICKS + g * GROUP + k] for k in range(GROUP)]
        gathered = jnp.concatenate(
            [state[pl.ds(2 * b, 2)].reshape(EDGE, MEMBERS) for b in chosen], axis=0
        )
        products = lax.dot_general(
            gathered, here, (((1,), (1,)), ((), ())), preferred_element_type=jnp.float32
        )
        for k, b in enumerate(chosen):
            d = spot[pl.ds(2 * b, 2)].reshape(EDGE, EDGE) - place
            damped = products[k * EDGE : (k + 1) * EDGE] * jnp.exp2(LIVE - d * d)
            tiles[k * EDGE : (k + 1) * EDGE] = damped.astype(jnp.bfloat16)

    def add_tiles(g):
        weight = weights(lists[BLOCKS + s * VISITS + g])
        chosen = [lists[s * PICKS + g * GROUP + k] for k in range(GROUP)]
        added = jnp.dot(tiles[...], weight, preferred_element_type=jnp.float32)
        for k, b in enumerate(chosen):
            acc[b] += added[k * EDGE : (k + 1) * EDGE]

    @pl.when(total > 0)
    def _():
        make_tiles(0)

        def step(g, carry):
            add_tiles(g - 1)
            make_tiles(g)
            return carry

        lax.fori_loop(1, total, step, 0)
        add_tiles(total - 1)


def split(ref):
    def part(i):
        t, r = lax.shift_right_logical(i, 2), jnp.bitwise_and(i, SPAN - 1)
        return ref[t, pl.ds(pl.multiple_of(r * EDGE, EDGE), EDGE), :]

    return part


def flat(ref, start):
    def part(i):
        return ref[pl.ds(pl.multiple_of(start + i * EDGE, PAD), EDGE), :]

    return part


def spread_places(held, places, start):
    places[start : start + SPAN] = held.astype(jnp.float32)[:SPAN] * STRETCH


def near_kernel(
    lists, s0, s1, s2, s3, oo, wo, ol, wl, orr, wr, state, spot, acc, places, tiles,
):
    column = lax.axis_index("obs")
    my_z = lax.shift_right_logical(column, 2)
    my_x = jnp.bitwise_and(column, NX - 1)
    lanes = lax.broadcasted_iota(jnp.int32, (SHARD, EDGE), 1)
    sublanes = lax.broadcasted_iota(jnp.int32, (SHARD, EDGE), 0)
    same = lanes == sublanes
    ones = jnp.ones((EDGE, EDGE), jnp.bfloat16)
    for k, piece in enumerate((s0, s1, s2, s3)):
        src_x = jnp.bitwise_and(my_x + (NX - k), NX - 1)
        held = piece[NZ * SHARD : NZ * SHARD + PAD, :EDGE].astype(jnp.float32)
        spread = jnp.concatenate(
            [jnp.where(same, held[p : p + 1], 0.0) for p in range(NZ)], axis=0
        ).astype(jnp.bfloat16)
        columns = jnp.dot(spread, ones, preferred_element_type=jnp.float32) * STRETCH
        for p, mask in enumerate(Z_ORDER):
            src = (my_z ^ mask) * NX + src_x
            state[src] = piece[p * SHARD : (p + 1) * SHARD, :]
            spot[src] = columns[p * SHARD : (p + 1) * SHARD]
    state[OBS:] = jnp.zeros((2, SHARD, MEMBERS), jnp.bfloat16)
    spot[OBS:] = jnp.zeros((2, SHARD, EDGE), jnp.float32)
    acc[...] = jnp.zeros_like(acc)
    for s, (o, w) in enumerate(((oo, wo), (ol, wl), (orr, wr))):
        for t in range(BATCHES):
            spread_places(o[t, OBS_ROWS : OBS_ROWS + PAD, :EDGE], places, t * SPAN)
        visit(s, split(o), split(w), places, state, spot, acc, tiles, lists)


def near(lists, arrays):
    return pl.pallas_call(
        near_kernel,
        out_shape=(
            jax.ShapeDtypeStruct((OBS + 2, SHARD, MEMBERS), jnp.bfloat16),
            jax.ShapeDtypeStruct((OBS + 2, SHARD, EDGE), jnp.float32),
            jax.ShapeDtypeStruct((RANGE_BLOCKS + 1, EDGE, MEMBERS), jnp.float32),
        ),
        in_specs=[SMEM] + [VMEM] * 10,
        out_specs=(VMEM,) * 3,
        scratch_shapes=[
            pltpu.VMEM((8, EDGE), jnp.float32),
            pltpu.VMEM((GROUP * EDGE, EDGE), jnp.bfloat16),
        ],
        compiler_params=pltpu.CompilerParams(vmem_limit_bytes=24 << 20),
        cost_estimate=pl.CostEstimate(
            flops=4_000_000_000, transcendentals=4_000_000, bytes_accessed=8_000_000
        ),
        name="near",
    )(lists, *arrays)


def far_kernel(lists, state, spot, near_acc, left, right, out, places, tiles, acc):
    acc[...] = near_acc[...]
    for s, both in ((3, left), (4, right)):
        spread_places(both[OBS_ROWS : OBS_ROWS + PAD, :EDGE], places, 0)
        visit(
            s, flat(both, 0), flat(both, OBS_ROWS + PAD), places, state, spot, acc, tiles, lists
        )
    out[...] = acc[:RANGE_BLOCKS].reshape(RANGE_BLOCKS * EDGE, MEMBERS).astype(jnp.bfloat16)


def far(lists, state, spot, acc, arrays):
    return pl.pallas_call(
        far_kernel,
        out_shape=jax.ShapeDtypeStruct((RANGE_BLOCKS * EDGE, MEMBERS), jnp.bfloat16),
        in_specs=[SMEM] + [VMEM] * 5,
        out_specs=VMEM,
        scratch_shapes=[
            pltpu.VMEM((8, EDGE), jnp.float32),
            pltpu.VMEM((GROUP * EDGE, EDGE), jnp.bfloat16),
            pltpu.VMEM((RANGE_BLOCKS + 1, EDGE, MEMBERS), jnp.float32),
        ],
        compiler_params=pltpu.CompilerParams(vmem_limit_bytes=24 << 20),
        cost_estimate=pl.CostEstimate(
            flops=1_000_000_000, transcendentals=1_000_000, bytes_accessed=8_000_000
        ),
        name="far",
    )(lists, state, spot, acc, *arrays)


def pack_kernel(a, b, out):
    held = SHARD + PAD
    places = []
    for p in range(NZ):
        ref, q = (a, p) if p < NZ // 2 else (b, p - NZ // 2)
        out[p * SHARD : (p + 1) * SHARD] = ref[q * held : q * held + SHARD]
        places.append(ref[q * held + SHARD : (q + 1) * held].astype(jnp.float32)[:1])
    places.append(jnp.zeros((PAD - NZ, MEMBERS), jnp.float32))
    out[NZ * SHARD :] = jnp.concatenate(places, axis=0).astype(jnp.bfloat16)


def pack(a, b):
    return pl.pallas_call(
        pack_kernel,
        out_shape=jax.ShapeDtypeStruct((NZ * SHARD + PAD, MEMBERS), jnp.bfloat16),
        in_specs=[VMEM, VMEM],
        out_specs=VMEM,
        compiler_params=pltpu.CompilerParams(vmem_limit_bytes=4 << 20),
        name="pack",
    )(a, b)


def join_kernel(*refs):
    out = refs[-1]
    start = 0
    for ref in refs[:-1]:
        out[start : start + ref.shape[0]] = ref[...]
        start += ref.shape[0]


def join(*parts):
    rows = sum(part.shape[0] for part in parts)
    return pl.pallas_call(
        join_kernel,
        out_shape=jax.ShapeDtypeStruct((rows, MEMBERS), jnp.bfloat16),
        in_specs=[VMEM] * len(parts),
        out_specs=VMEM,
        compiler_params=pltpu.CompilerParams(vmem_limit_bytes=4 << 20),
        name="join",
    )(*parts)


def load_kernel(obs, places, out):
    for t in range(BATCHES):
        out[t, :OBS_ROWS] = obs[t]
        held = places[t : t + 1].astype(jnp.float32)
        rows = [held[:, r * EDGE : (r + 1) * EDGE] for r in range(SPAN)]
        rows.append(jnp.zeros((PAD - SPAN, EDGE), jnp.float32))
        out[t, OBS_ROWS:, :EDGE] = jnp.concatenate(rows, axis=0).astype(jnp.bfloat16)
        out[t, OBS_ROWS:, EDGE:] = jnp.zeros((PAD, MEMBERS - EDGE), jnp.bfloat16)


def load(obs, places):
    return pl.pallas_call(
        load_kernel,
        out_shape=jax.ShapeDtypeStruct((BATCHES, OBS_ROWS + PAD, MEMBERS), jnp.bfloat16),
        in_specs=[VMEM, VMEM],
        out_specs=VMEM,
        compiler_params=pltpu.CompilerParams(vmem_limit_bytes=8 << 20),
        name="load",
    )(obs, places)


def relay_kernel(batch, obs, weights, out):
    out[: OBS_ROWS + PAD] = obs[batch]
    out[OBS_ROWS + PAD :] = weights[batch]


def relay(batch, obs, weights):
    return pl.pallas_call(
        functools.partial(relay_kernel, batch),
        out_shape=jax.ShapeDtypeStruct((2 * OBS_ROWS + PAD, MEMBERS), jnp.bfloat16),
        in_specs=[VMEM, VMEM],
        out_specs=VMEM,
        compiler_params=pltpu.CompilerParams(vmem_limit_bytes=8 << 20),
        name="relay",
    )(obs, weights)


def local(ens_state, state_pos, obs_ens, obs_pos, innov_weight, block_rows):
    state = jnp.concatenate(
        [ens_state[0], jnp.pad(state_pos[None, :], ((0, PAD - 1), (0, MEMBERS - SHARD)))], axis=0
    )
    mine = flip(state)
    parts = [mine]
    for mask in (4, 2, 6):
        parts.append(swap_z_flip(state, mask))
    state = join(*parts)
    other = swap_z(state, 1)
    state = pack(state, other)
    pieces = [state]
    for k in range(1, NX):
        pieces.append(along_x(state, k))

    weight = innov_weight[:, 0]
    weight_left = along_rows(weight, 1)
    weight_right = along_rows(weight, ROWS - 1)
    obs = load(obs_ens[:, 0], obs_pos)
    obs_left = along_rows_flip(obs, 1)
    obs_right = along_rows_flip(obs, ROWS - 1)
    obs_own = flip(obs)
    far0 = relay(0, obs_left, weight_left)
    far0 = along_rows(far0, 1)
    far1 = relay(1, obs_right, weight_right)
    far1 = along_rows(far1, ROWS - 1)

    lists = make_lists(jnp.transpose(block_rows, (0, 2, 1)))
    held = near(lists, (*pieces, obs_own, weight, obs_left, weight_left, obs_right, weight_right))
    partial = far(lists, *held, (far0, far1))
    shares = lax.all_to_all(partial, "obs", 0, 0, tiled=True)
    shares = shares.reshape(OBS, SHARD, MEMBERS).astype(jnp.float32)
    return jnp.sum(shares, axis=0)[None]


def solution(mesh):
    in_specs = (
        P("half", ("rows", "obs"), None),
        P(("rows", "obs")),
        P(None, "half", ("rows", "obs"), None),
        P(None, ("rows", "obs")),
        P(None, "half", ("rows", "obs"), None),
        P(),
    )
    out_specs = P("half", ("rows", "obs"), None)
    return jax.shard_map(local, mesh=mesh, in_specs=in_specs, out_specs=out_specs, check_vma=False)
```

```python
import functools
import math

import jax
import jax.numpy as jnp
from jax import lax
from jax.experimental import pallas as pl
from jax.experimental.pallas import tpu as pltpu
from jax.sharding import PartitionSpec as P


BATCHES = 2
ROWS, HALVES, OBS = 4, 2, 32
NX, NZ = 4, 8
EDGE = 128
SHARD = 64
MEMBERS = 256
RANGE_BLOCKS = 16
SPAN = 4
NAMED = 16
OBS_ROWS = SPAN * EDGE
PAD = 16
Z_ORDER = (0, 4, 2, 6, 1, 5, 3, 7)

GROUP = 8
SOURCES = ((0, 2, 0), (3, 2, 0), (1, 2, 0), (2, 1, 0), (2, 1, 1))
PICKS = 10 * GROUP + NAMED
VISITS = 10
BLOCKS = len(SOURCES) * PICKS
TOTALS = BLOCKS + len(SOURCES) * VISITS + 8
LIVE = math.log2(1.0 / (MEMBERS - 1))
STRETCH = 2.0 * math.sqrt(math.log2(math.e))

VMEM = pl.BlockSpec(memory_space=pltpu.VMEM)
SMEM = pl.BlockSpec(memory_space=pltpu.SMEM)


def flip(value):
    return lax.ppermute(value, "half", [(0, 1), (1, 0)])


def along_rows(value, step):
    return lax.ppermute(value, "rows", [(s, (s + step) % ROWS) for s in range(ROWS)])


def along_rows_flip(value, step):
    pairs = [
        (r * HALVES + h, ((r + step) % ROWS) * HALVES + 1 - h)
        for r in range(ROWS)
        for h in range(HALVES)
    ]
    return lax.ppermute(value, ("rows", "half"), pairs)


def swap_z(value, mask):
    pairs = [(z * NX + x, (z ^ mask) * NX + x) for z in range(NZ) for x in range(NX)]
    return lax.ppermute(value, "obs", pairs)


def swap_z_flip(value, mask):
    pairs = [
        (h * OBS + z * NX + x, (1 - h) * OBS + (z ^ mask) * NX + x)
        for h in range(HALVES)
        for z in range(NZ)
        for x in range(NX)
    ]
    return lax.ppermute(value, ("half", "obs"), pairs)


def swap_x(value, mask):
    pairs = [(z * NX + x, z * NX + (x ^ mask)) for z in range(NZ) for x in range(NX)]
    return lax.ppermute(value, "obs", pairs)


def along_x(value, step):
    pairs = [(z * NX + x, z * NX + (x + step) % NX) for z in range(NZ) for x in range(NX)]
    return lax.ppermute(value, "obs", pairs)


def lists_kernel(named_ref, lists):
    row, column = lax.axis_index("rows"), lax.axis_index("obs")
    first = row * RANGE_BLOCKS
    for s, (turn, batches, batch) in enumerate(SOURCES):
        owner = jnp.bitwise_and(row + turn, ROWS - 1) * OBS + column

        def fill(i, visits, s=s, batch=batch, owner=owner):
            t = batch + lax.shift_right_logical(i, 2)
            place = owner * SPAN + jnp.bitwise_and(i, SPAN - 1)
            start = s * PICKS + visits * GROUP
            for k in range(GROUP):
                lists[start + k] = RANGE_BLOCKS
            write = start
            for e in range(NAMED):
                relative = named_ref[t, e, place] - first
                inside = jnp.bitwise_and(relative, -RANGE_BLOCKS) == 0
                lists[write] = jnp.where(inside, relative, RANGE_BLOCKS)
                write = write + inside.astype(jnp.int32)
            lists[BLOCKS + s * VISITS + visits] = i
            return visits + (write > start).astype(jnp.int32)

        visits = lax.fori_loop(0, batches * SPAN, fill, jnp.int32(0))
        lists[TOTALS + s] = visits
        lists[BLOCKS + s * VISITS + visits] = 0
        for k in range(GROUP):
            lists[s * PICKS + visits * GROUP + k] = RANGE_BLOCKS


def make_lists(named):
    return pl.pallas_call(
        lists_kernel,
        out_shape=jax.ShapeDtypeStruct((TOTALS + 8,), jnp.int32),
        in_specs=[SMEM],
        out_specs=SMEM,
        compiler_params=pltpu.CompilerParams(vmem_limit_bytes=1 << 20),
        cost_estimate=pl.CostEstimate(flops=4_000_000, transcendentals=0, bytes_accessed=4_000_000),
        name="lists",
    )(named)


def visit(s, obs, weights, places, state, spot, acc, tiles, lists):
    total = lists[TOTALS + s]

    def make_tiles(g, lane):
        i = lists[BLOCKS + s * VISITS + g]
        here = obs(i)
        place = places[pl.ds(i, 1), :]
        chosen = [lists[s * PICKS + g * GROUP + k] for k in range(GROUP)]
        gathered = jnp.concatenate(
            [state[pl.ds(2 * b, 2)].reshape(EDGE, MEMBERS) for b in chosen], axis=0
        )
        products = lax.dot_general(
            gathered, here, (((1,), (1,)), ((), ())), preferred_element_type=jnp.float32
        )
        for k, b in enumerate(chosen):
            d = spot[pl.ds(2 * b, 2)].reshape(EDGE, EDGE) - place
            damped = products[k * EDGE : (k + 1) * EDGE] * jnp.exp2(LIVE - d * d)
            tiles[lane, k * EDGE : (k + 1) * EDGE] = damped.astype(jnp.bfloat16)

    def add_tiles(g, lane):
        weight = weights(lists[BLOCKS + s * VISITS + g])
        chosen = [lists[s * PICKS + g * GROUP + k] for k in range(GROUP)]
        added = jnp.dot(tiles[lane], weight, preferred_element_type=jnp.float32)
        for k, b in enumerate(chosen):
            acc[b] += added[k * EDGE : (k + 1) * EDGE]

    @pl.when(total > 0)
    def _():
        make_tiles(0, 0)
        make_tiles(1, 1)

        def step(h, carry):
            g = 2 * h
            add_tiles(g - 2, 0)
            make_tiles(g, 0)
            add_tiles(g - 1, 1)
            make_tiles(g + 1, 1)
            return carry

        pairs = lax.shift_right_logical(total + 1, 1)
        lax.fori_loop(1, pairs, step, 0)
        add_tiles(2 * pairs - 2, 0)
        add_tiles(2 * pairs - 1, 1)


def split(ref):
    def part(i):
        t, r = lax.shift_right_logical(i, 2), jnp.bitwise_and(i, SPAN - 1)
        return ref[t, pl.ds(pl.multiple_of(r * EDGE, EDGE), EDGE), :]

    return part


def flat(ref, start):
    def part(i):
        return ref[pl.ds(pl.multiple_of(start + i * EDGE, PAD), EDGE), :]

    return part


def spread_places(held, places, start):
    places[start : start + SPAN] = held.astype(jnp.float32)[:SPAN] * STRETCH


def near_kernel(
    lists, s0, s1, s2, s3, oo, wo, ol, wl, orr, wr, state, spot, acc, places, tiles,
):
    column = lax.axis_index("obs")
    my_z = lax.shift_right_logical(column, 2)
    my_x = jnp.bitwise_and(column, NX - 1)
    lanes = lax.broadcasted_iota(jnp.int32, (SHARD, EDGE), 1)
    sublanes = lax.broadcasted_iota(jnp.int32, (SHARD, EDGE), 0)
    same = lanes == sublanes
    ones = jnp.ones((EDGE, EDGE), jnp.bfloat16)
    for k, piece in enumerate((s0, s1, s2, s3)):
        src_x = jnp.bitwise_and(my_x + (NX - k), NX - 1)
        held = piece[NZ * SHARD : NZ * SHARD + PAD, :EDGE].astype(jnp.float32)
        spread = jnp.concatenate(
            [jnp.where(same, held[p : p + 1], 0.0) for p in range(NZ)], axis=0
        ).astype(jnp.bfloat16)
        columns = jnp.dot(spread, ones, preferred_element_type=jnp.float32) * STRETCH
        for p, mask in enumerate(Z_ORDER):
            src = (my_z ^ mask) * NX + src_x
            state[src] = piece[p * SHARD : (p + 1) * SHARD, :]
            spot[src] = columns[p * SHARD : (p + 1) * SHARD]
    state[OBS:] = jnp.zeros((2, SHARD, MEMBERS), jnp.bfloat16)
    spot[OBS:] = jnp.zeros((2, SHARD, EDGE), jnp.float32)
    acc[...] = jnp.zeros_like(acc)
    for s, (o, w) in enumerate(((oo, wo), (ol, wl), (orr, wr))):
        for t in range(BATCHES):
            spread_places(o[t, OBS_ROWS : OBS_ROWS + PAD, :EDGE], places, t * SPAN)
        visit(s, split(o), split(w), places, state, spot, acc, tiles, lists)


def near(lists, arrays):
    return pl.pallas_call(
        near_kernel,
        out_shape=(
            jax.ShapeDtypeStruct((OBS + 2, SHARD, MEMBERS), jnp.bfloat16),
            jax.ShapeDtypeStruct((OBS + 2, SHARD, EDGE), jnp.float32),
            jax.ShapeDtypeStruct((RANGE_BLOCKS + 1, EDGE, MEMBERS), jnp.float32),
        ),
        in_specs=[SMEM] + [VMEM] * 10,
        out_specs=(VMEM,) * 3,
        scratch_shapes=[
            pltpu.VMEM((8, EDGE), jnp.float32),
            pltpu.VMEM((2, GROUP * EDGE, EDGE), jnp.bfloat16),
        ],
        compiler_params=pltpu.CompilerParams(vmem_limit_bytes=24 << 20),
        cost_estimate=pl.CostEstimate(
            flops=4_000_000_000, transcendentals=4_000_000, bytes_accessed=8_000_000
        ),
        name="near",
    )(lists, *arrays)


def far_kernel(lists, state, spot, near_acc, left, right, own, x1, x2, x3, places, tiles, acc):
    acc[...] = near_acc[...]
    for s, both in ((3, left), (4, right)):
        spread_places(both[OBS_ROWS : OBS_ROWS + PAD, :EDGE], places, 0)
        visit(
            s, flat(both, 0), flat(both, OBS_ROWS + PAD), places, state, spot, acc, tiles, lists
        )
    my_x = jnp.bitwise_and(lax.axis_index("obs"), NX - 1)
    for mask, out in enumerate((own, x1, x2, x3)):
        x = jnp.bitwise_xor(my_x, mask)
        start = pl.multiple_of(jnp.bitwise_and(x, 1) * SHARD, SHARD)
        for z in range(NZ):
            block = 2 * z + lax.shift_right_logical(x, 1)
            part = acc[block, pl.ds(start, SHARD), :]
            out[z * SHARD : (z + 1) * SHARD] = part.astype(out.dtype)


def far(lists, state, spot, acc, arrays):
    rows = NZ * SHARD
    return pl.pallas_call(
        far_kernel,
        out_shape=(jax.ShapeDtypeStruct((rows, MEMBERS), jnp.float32),)
        + (jax.ShapeDtypeStruct((rows, MEMBERS), jnp.bfloat16),) * 3,
        in_specs=[SMEM] + [VMEM] * 5,
        out_specs=(VMEM,) * 4,
        scratch_shapes=[
            pltpu.VMEM((8, EDGE), jnp.float32),
            pltpu.VMEM((2, GROUP * EDGE, EDGE), jnp.bfloat16),
            pltpu.VMEM((RANGE_BLOCKS + 1, EDGE, MEMBERS), jnp.float32),
        ],
        compiler_params=pltpu.CompilerParams(vmem_limit_bytes=24 << 20),
        cost_estimate=pl.CostEstimate(
            flops=1_000_000_000, transcendentals=1_000_000, bytes_accessed=8_000_000
        ),
        name="far",
    )(lists, state, spot, acc, *arrays)


def sum_x_kernel(own, x1, x2, x3, keep, send):
    my_z = lax.shift_right_logical(lax.axis_index("obs"), 2)
    for mask in range(NZ):
        rows = pl.ds(pl.multiple_of(jnp.bitwise_xor(my_z, mask) * SHARD, SHARD), SHARD)
        total = own[rows, :]
        for ref in (x1, x2, x3):
            total += ref[rows, :].astype(jnp.float32)
        out, k = (send if mask & 1 else keep), mask // 2
        out[k * SHARD : (k + 1) * SHARD] = total


def sum_z1_kernel(keep, got, own, z2, z4, z6):
    for k, out in enumerate((own, z2, z4, z6)):
        rows = slice(k * SHARD, (k + 1) * SHARD)
        out[...] = keep[rows] + got[rows]


def sum_z_kernel(own, z2, z4, z6, out):
    out[...] = own[...] + z2[...] + z4[...] + z6[...]


def small(body, out_rows, *arrays):
    return pl.pallas_call(
        body,
        out_shape=tuple(jax.ShapeDtypeStruct((r, MEMBERS), jnp.float32) for r in out_rows),
        in_specs=[VMEM] * len(arrays),
        out_specs=(VMEM,) * len(out_rows),
        compiler_params=pltpu.CompilerParams(vmem_limit_bytes=6 << 20),
    )(*arrays)


def pack_kernel(a, b, out):
    held = SHARD + PAD
    places = []
    for p in range(NZ):
        ref, q = (a, p) if p < NZ // 2 else (b, p - NZ // 2)
        out[p * SHARD : (p + 1) * SHARD] = ref[q * held : q * held + SHARD]
        places.append(ref[q * held + SHARD : (q + 1) * held].astype(jnp.float32)[:1])
    places.append(jnp.zeros((PAD - NZ, MEMBERS), jnp.float32))
    out[NZ * SHARD :] = jnp.concatenate(places, axis=0).astype(jnp.bfloat16)


def pack(a, b):
    return pl.pallas_call(
        pack_kernel,
        out_shape=jax.ShapeDtypeStruct((NZ * SHARD + PAD, MEMBERS), jnp.bfloat16),
        in_specs=[VMEM, VMEM],
        out_specs=VMEM,
        compiler_params=pltpu.CompilerParams(vmem_limit_bytes=4 << 20),
        name="pack",
    )(a, b)


def join_kernel(*refs):
    out = refs[-1]
    start = 0
    for ref in refs[:-1]:
        out[start : start + ref.shape[0]] = ref[...]
        start += ref.shape[0]


def join(*parts):
    rows = sum(part.shape[0] for part in parts)
    return pl.pallas_call(
        join_kernel,
        out_shape=jax.ShapeDtypeStruct((rows, MEMBERS), jnp.bfloat16),
        in_specs=[VMEM] * len(parts),
        out_specs=VMEM,
        compiler_params=pltpu.CompilerParams(vmem_limit_bytes=4 << 20),
        name="join",
    )(*parts)


def load_kernel(obs, places, out):
    for t in range(BATCHES):
        out[t, :OBS_ROWS] = obs[t]
        held = places[t : t + 1].astype(jnp.float32)
        rows = [held[:, r * EDGE : (r + 1) * EDGE] for r in range(SPAN)]
        rows.append(jnp.zeros((PAD - SPAN, EDGE), jnp.float32))
        out[t, OBS_ROWS:, :EDGE] = jnp.concatenate(rows, axis=0).astype(jnp.bfloat16)
        out[t, OBS_ROWS:, EDGE:] = jnp.zeros((PAD, MEMBERS - EDGE), jnp.bfloat16)


def load(obs, places):
    return pl.pallas_call(
        load_kernel,
        out_shape=jax.ShapeDtypeStruct((BATCHES, OBS_ROWS + PAD, MEMBERS), jnp.bfloat16),
        in_specs=[VMEM, VMEM],
        out_specs=VMEM,
        compiler_params=pltpu.CompilerParams(vmem_limit_bytes=8 << 20),
        name="load",
    )(obs, places)


def relay_kernel(batch, obs, weights, out):
    out[: OBS_ROWS + PAD] = obs[batch]
    out[OBS_ROWS + PAD :] = weights[batch]


def relay(batch, obs, weights):
    return pl.pallas_call(
        functools.partial(relay_kernel, batch),
        out_shape=jax.ShapeDtypeStruct((2 * OBS_ROWS + PAD, MEMBERS), jnp.bfloat16),
        in_specs=[VMEM, VMEM],
        out_specs=VMEM,
        compiler_params=pltpu.CompilerParams(vmem_limit_bytes=8 << 20),
        name="relay",
    )(obs, weights)


def local(ens_state, state_pos, obs_ens, obs_pos, innov_weight, block_rows):
    state = jnp.concatenate(
        [ens_state[0], jnp.pad(state_pos[None, :], ((0, PAD - 1), (0, MEMBERS - SHARD)))], axis=0
    )
    mine = flip(state)
    parts = [mine]
    for mask in (4, 2, 6):
        parts.append(swap_z_flip(state, mask))
    state = join(*parts)
    other = swap_z(state, 1)
    state = pack(state, other)
    pieces = [state]
    for k in range(1, NX):
        pieces.append(along_x(state, k))

    weight = innov_weight[:, 0]
    weight_left = along_rows(weight, 1)
    weight_right = along_rows(weight, ROWS - 1)
    obs = load(obs_ens[:, 0], obs_pos)
    obs_left = along_rows_flip(obs, 1)
    obs_right = along_rows_flip(obs, ROWS - 1)
    obs_own = flip(obs)
    far0 = relay(0, obs_left, weight_left)
    far0 = along_rows(far0, 1)
    far1 = relay(1, obs_right, weight_right)
    far1 = along_rows(far1, ROWS - 1)

    lists = make_lists(jnp.transpose(block_rows, (0, 2, 1)))
    held = near(lists, (*pieces, obs_own, weight, obs_left, weight_left, obs_right, weight_right))
    own, *parts = far(lists, *held, (far0, far1))
    for mask in (2, 1, 3):
        parts[mask - 1] = swap_x(parts[mask - 1], mask)
    keep, send = small(sum_x_kernel, (4 * SHARD, 4 * SHARD), own, *parts)
    got = swap_z(send, 1)
    own, *parts = small(sum_z1_kernel, (SHARD,) * 4, keep, got)
    for k, mask in ((1, 4), (0, 2), (2, 6)):
        parts[k] = swap_z(parts[k], mask)
    (total,) = small(sum_z_kernel, (SHARD,), own, *parts)
    return total[None]


def solution(mesh):
    in_specs = (
        P("half", ("rows", "obs"), None),
        P(("rows", "obs")),
        P(None, "half", ("rows", "obs"), None),
        P(None, ("rows", "obs")),
        P(None, "half", ("rows", "obs"), None),
        P(),
    )
    out_specs = P("half", ("rows", "obs"), None)
    return jax.shard_map(local, mesh=mesh, in_specs=in_specs, out_specs=out_specs, check_vma=False)
```

```python
import functools
import math

import jax
import jax.numpy as jnp
from jax import lax
from jax.experimental import pallas as pl
from jax.experimental.pallas import tpu as pltpu
from jax.sharding import PartitionSpec as P


BATCHES = 2
ROWS, HALVES, OBS = 4, 2, 32
NX, NZ = 4, 8
EDGE = 128
SHARD = 64
MEMBERS = 256
RANGE_BLOCKS = 16
SPAN = 4
NAMED = 16
OBS_ROWS = SPAN * EDGE
PAD = 16
Z_ORDER = (0, 4, 2, 6, 1, 5, 3, 7)

GROUP = 4
SPANS = 8
SOURCES = 5
PICKS = 24
META = SOURCES * 2 * PICKS
TOTALS = META + SOURCES * 2 * 8
KEYS = RANGE_BLOCKS + 2
TURNS = 0b10_01_11_00
DEAD = -1e30
LIVE = math.log2(1.0 / (MEMBERS - 1))
STRETCH = 2.0 * math.sqrt(math.log2(math.e))

VMEM = pl.BlockSpec(memory_space=pltpu.VMEM)
SMEM = pl.BlockSpec(memory_space=pltpu.SMEM)


def flip(value):
    return lax.ppermute(value, "half", [(0, 1), (1, 0)])


def along_rows(value, step):
    return lax.ppermute(value, "rows", [(s, (s + step) % ROWS) for s in range(ROWS)])


def along_rows_flip(value, step):
    pairs = [
        (r * HALVES + h, ((r + step) % ROWS) * HALVES + 1 - h)
        for r in range(ROWS)
        for h in range(HALVES)
    ]
    return lax.ppermute(value, ("rows", "half"), pairs)


def swap_z(value, mask):
    pairs = [(z * NX + x, (z ^ mask) * NX + x) for z in range(NZ) for x in range(NX)]
    return lax.ppermute(value, "obs", pairs)


def swap_z_flip(value, mask):
    pairs = [
        (h * OBS + z * NX + x, (1 - h) * OBS + (z ^ mask) * NX + x)
        for h in range(HALVES)
        for z in range(NZ)
        for x in range(NX)
    ]
    return lax.ppermute(value, ("half", "obs"), pairs)


def swap_x(value, mask):
    pairs = [(z * NX + x, z * NX + (x ^ mask)) for z in range(NZ) for x in range(NX)]
    return lax.ppermute(value, "obs", pairs)


def lists_kernel(named_ref, lists, shifts, used):
    row, column = lax.axis_index("rows"), lax.axis_index("obs")
    first = row * RANGE_BLOCKS

    def span(n, carry):
        near_side = n < 6
        source = jnp.where(near_side, lax.shift_right_logical(n, 1), n - 3)
        local_t = jnp.where(near_side, jnp.bitwise_and(n, 1), 0)
        turn = jnp.bitwise_and(
            lax.shift_right_logical(TURNS, 2 * lax.shift_right_logical(n, 1)), ROWS - 1
        )
        place = (jnp.bitwise_and(row + turn, ROWS - 1) * OBS + column) * SPAN
        batch = jnp.bitwise_and(n, 1)
        key = n * KEYS
        for k in range(KEYS):
            used[key + k] = 0
            for j in range(SPAN):
                shifts[(key + k) * SPAN + j] = DEAD
        for j in range(SPAN):
            for e in range(NAMED):
                relative = named_ref[batch, e, place + j] - first
                inside = jnp.bitwise_and(relative, -RANGE_BLOCKS) == 0
                at = jnp.where(inside, key + relative, SPANS * KEYS)
                used[at] = 1
                shifts[at * SPAN + j] = LIVE
        for parity in range(2):
            r = source * 2 + parity
            before = jnp.where(local_t == 0, 0, lists[TOTALS + r])
            start = r * PICKS + before * GROUP
            write = start
            for z in range(NZ):
                lists[write] = z
                write = write + used[key + 2 * z + parity]
            for k in range(GROUP - 1):
                lists[write + k] = NZ
            visits = lax.shift_right_logical(write - start + GROUP - 1, 2)
            for k in range(2):
                lists[META + r * 8 + before + k] = local_t
            total = before + visits

            @pl.when(total == 0)
            def _(start=start):
                for k in range(GROUP):
                    lists[start + k] = NZ

            last = jnp.logical_or(local_t == 1, jnp.logical_not(near_side))
            lists[TOTALS + r] = jnp.where(last, jnp.maximum(total, 1), total)
        return carry

    lax.fori_loop(0, SPANS, span, 0)


def make_lists(named):
    return pl.pallas_call(
        lists_kernel,
        out_shape=(
            jax.ShapeDtypeStruct((TOTALS + 16,), jnp.int32),
            jax.ShapeDtypeStruct(((SPANS * KEYS + 1) * SPAN,), jnp.float32),
        ),
        in_specs=[SMEM],
        out_specs=(SMEM, SMEM),
        scratch_shapes=[pltpu.SMEM((SPANS * KEYS + 1,), jnp.int32)],
        compiler_params=pltpu.CompilerParams(vmem_limit_bytes=1 << 20),
        cost_estimate=pl.CostEstimate(flops=4_000_000, transcendentals=0, bytes_accessed=4_000_000),
        name="lists",
    )(named)


def tile_loop(segments, parity, state, spot, acc, places, tiles, lists, shifts):
    def chosen(s, g):
        return [lists[(s * 2 + parity) * PICKS + g * GROUP + k] for k in range(GROUP)]

    def batch_of(s, g):
        return lists[META + (s * 2 + parity) * 8 + g]

    def make(segment, g):
        s, n, rows, obs, _ = segment
        t = batch_of(s, g)
        picks = chosen(s, g)
        gathered = jnp.concatenate(
            [state[pl.ds(2 * z, 2)].reshape(EDGE, MEMBERS) for z in picks], axis=0
        )
        products = lax.dot_general(
            gathered, obs(t), (((1,), (1,)), ((), ())), preferred_element_type=jnp.float32
        )
        for k, z in enumerate(picks):
            key = ((n + t) * KEYS + 2 * z + parity) * SPAN
            positions = spot[pl.ds(2 * z, 2)].reshape(EDGE, EDGE)
            for j in range(SPAN):
                d = positions - places[pl.ds(rows + t * SPAN + j, 1), :]
                part = products[k * EDGE : (k + 1) * EDGE, j * EDGE : (j + 1) * EDGE]
                damped = part * jnp.exp2(shifts[key + j] - d * d)
                tiles[k * EDGE : (k + 1) * EDGE, j * EDGE : (j + 1) * EDGE] = damped.astype(
                    jnp.bfloat16
                )

    def add(segment, g):
        s, weights = segment[0], segment[4]
        added = jnp.dot(
            tiles[...], weights(batch_of(s, g)), preferred_element_type=jnp.float32
        )
        for k, z in enumerate(chosen(s, g)):
            acc[z] += added[k * EDGE : (k + 1) * EDGE]

    before = None
    for segment in segments:
        total = lists[TOTALS + segment[0] * 2 + parity]
        if before is not None:
            add(*before)
        make(segment, 0)

        def step(g, carry, segment=segment):
            add(segment, g - 1)
            make(segment, g)
            return carry

        lax.fori_loop(1, total, step, 0)
        before = (segment, total - 1)
    add(*before)


def spread_places(held, places, start):
    places[start : start + SPAN] = held.astype(jnp.float32)[:SPAN] * STRETCH


def own_place(late):
    column = lax.axis_index("obs")
    my_z = lax.shift_right_logical(column, 2)
    x = jnp.bitwise_xor(jnp.bitwise_and(column, NX - 1), 2 * late)
    return my_z, x


def near_kernel(
    late, lists, shifts, p0, p1, oo, wo, ol, wl, orr, wr, state, spot, acc, places, tiles
):
    my_z, x = own_place(late)
    lanes = lax.broadcasted_iota(jnp.int32, (SHARD, EDGE), 1)
    sublanes = lax.broadcasted_iota(jnp.int32, (SHARD, EDGE), 0)
    same = lanes == sublanes
    ones = jnp.ones((EDGE, EDGE), jnp.bfloat16)
    for k, piece in enumerate((p0, p1)):
        half = jnp.bitwise_and(jnp.bitwise_xor(x, k), 1)
        held = piece[NZ * SHARD : NZ * SHARD + PAD, :EDGE].astype(jnp.float32)
        spread = jnp.concatenate(
            [jnp.where(same, held[p : p + 1], 0.0) for p in range(NZ)], axis=0
        ).astype(jnp.bfloat16)
        columns = jnp.dot(spread, ones, preferred_element_type=jnp.float32) * STRETCH
        for p, mask in enumerate(Z_ORDER):
            at = jnp.bitwise_xor(my_z, mask) * 2 + half
            state[at] = piece[p * SHARD : (p + 1) * SHARD, :]
            spot[at] = columns[p * SHARD : (p + 1) * SHARD]
    state[2 * NZ :] = jnp.zeros((2, SHARD, MEMBERS), jnp.bfloat16)
    spot[2 * NZ :] = jnp.zeros((2, SHARD, EDGE), jnp.float32)
    acc[...] = jnp.zeros_like(acc)
    segments = []
    for s, (o, w) in enumerate(((oo, wo), (ol, wl), (orr, wr))):
        for t in range(BATCHES):
            spread_places(o[t, OBS_ROWS : OBS_ROWS + PAD, :EDGE], places, s * 8 + t * SPAN)
        segments.append(
            (s, 2 * s, 8 * s, lambda t, o=o: o[t, :OBS_ROWS, :], lambda t, w=w: w[t])
        )
    parity = lax.shift_right_logical(x, 1)
    tile_loop(segments, parity, state, spot, acc, places, tiles, lists, shifts)


SCRATCH = [
    pltpu.VMEM((24, EDGE), jnp.float32),
    pltpu.VMEM((GROUP * EDGE, SPAN * EDGE), jnp.bfloat16),
]


def near(late, lists, arrays):
    return pl.pallas_call(
        functools.partial(near_kernel, late),
        out_shape=(
            jax.ShapeDtypeStruct((2 * NZ + 2, SHARD, MEMBERS), jnp.bfloat16),
            jax.ShapeDtypeStruct((2 * NZ + 2, SHARD, EDGE), jnp.float32),
            jax.ShapeDtypeStruct((NZ + 1, EDGE, MEMBERS), jnp.float32),
        ),
        in_specs=[SMEM, SMEM] + [VMEM] * 8,
        out_specs=(VMEM,) * 3,
        scratch_shapes=SCRATCH,
        compiler_params=pltpu.CompilerParams(vmem_limit_bytes=16 << 20),
        cost_estimate=pl.CostEstimate(
            flops=2_000_000_000, transcendentals=2_000_000, bytes_accessed=4_000_000
        ),
        name="near_late" if late else "near_early",
    )(*lists, *arrays)


def far_kernel(
    late, lists, shifts, state, spot, near_acc, left, right, r0, r1, places, tiles, acc
):
    acc[...] = near_acc[...]
    segments = []
    for k, both in enumerate((left, right)):
        spread_places(both[OBS_ROWS : OBS_ROWS + PAD, :EDGE], places, 8 * k)
        segments.append(
            (
                3 + k, 6 + k, 8 * k, lambda t, both=both: both[:OBS_ROWS, :],
                lambda t, both=both: both[OBS_ROWS + PAD :, :],
            )
        )
    _, x = own_place(late)
    parity = lax.shift_right_logical(x, 1)
    tile_loop(segments, parity, state, spot, acc, places, tiles, lists, shifts)
    for k, out in enumerate((r0, r1)):
        half = jnp.bitwise_and(jnp.bitwise_xor(x, k), 1)
        start = pl.multiple_of(half * SHARD, SHARD)
        for z in range(NZ):
            out[z * SHARD : (z + 1) * SHARD] = acc[z, pl.ds(start, SHARD), :].astype(out.dtype)


def far(late, lists, state, spot, acc, arrays):
    rows = NZ * SHARD
    return pl.pallas_call(
        functools.partial(far_kernel, late),
        out_shape=(
            jax.ShapeDtypeStruct((rows, MEMBERS), jnp.bfloat16 if late else jnp.float32),
            jax.ShapeDtypeStruct((rows, MEMBERS), jnp.bfloat16),
        ),
        in_specs=[SMEM, SMEM] + [VMEM] * 5,
        out_specs=(VMEM, VMEM),
        scratch_shapes=SCRATCH + [pltpu.VMEM((NZ + 1, EDGE, MEMBERS), jnp.float32)],
        compiler_params=pltpu.CompilerParams(vmem_limit_bytes=16 << 20),
        cost_estimate=pl.CostEstimate(
            flops=500_000_000, transcendentals=500_000, bytes_accessed=4_000_000
        ),
        name="far_late" if late else "far_early",
    )(*lists, state, spot, acc, *arrays)


def sum_x_kernel(own, x1, x2, x3, keep, send):
    my_z = lax.shift_right_logical(lax.axis_index("obs"), 2)
    for mask in range(NZ):
        rows = pl.ds(pl.multiple_of(jnp.bitwise_xor(my_z, mask) * SHARD, SHARD), SHARD)
        total = own[rows, :]
        for ref in (x1, x2, x3):
            total += ref[rows, :].astype(jnp.float32)
        out, k = (send if mask & 1 else keep), mask // 2
        out[k * SHARD : (k + 1) * SHARD] = total


def sum_z1_kernel(keep, got, own, z2, z4, z6):
    for k, out in enumerate((own, z2, z4, z6)):
        rows = slice(k * SHARD, (k + 1) * SHARD)
        out[...] = keep[rows] + got[rows]


def sum_z_kernel(own, z2, z4, z6, out):
    out[...] = own[...] + z2[...] + z4[...] + z6[...]


def small(body, out_rows, *arrays):
    return pl.pallas_call(
        body,
        out_shape=tuple(jax.ShapeDtypeStruct((r, MEMBERS), jnp.float32) for r in out_rows),
        in_specs=[VMEM] * len(arrays),
        out_specs=(VMEM,) * len(out_rows),
        compiler_params=pltpu.CompilerParams(vmem_limit_bytes=6 << 20),
    )(*arrays)


def pack_kernel(a, b, out):
    held = SHARD + PAD
    places = []
    for p in range(NZ):
        ref, q = (a, p) if p < NZ // 2 else (b, p - NZ // 2)
        out[p * SHARD : (p + 1) * SHARD] = ref[q * held : q * held + SHARD]
        places.append(ref[q * held + SHARD : (q + 1) * held].astype(jnp.float32)[:1])
    places.append(jnp.zeros((PAD - NZ, MEMBERS), jnp.float32))
    out[NZ * SHARD :] = jnp.concatenate(places, axis=0).astype(jnp.bfloat16)


def pack(a, b):
    return pl.pallas_call(
        pack_kernel,
        out_shape=jax.ShapeDtypeStruct((NZ * SHARD + PAD, MEMBERS), jnp.bfloat16),
        in_specs=[VMEM, VMEM],
        out_specs=VMEM,
        compiler_params=pltpu.CompilerParams(vmem_limit_bytes=4 << 20),
        name="pack",
    )(a, b)


def join_kernel(*refs):
    out = refs[-1]
    start = 0
    for ref in refs[:-1]:
        out[start : start + ref.shape[0]] = ref[...]
        start += ref.shape[0]


def join(*parts):
    rows = sum(part.shape[0] for part in parts)
    return pl.pallas_call(
        join_kernel,
        out_shape=jax.ShapeDtypeStruct((rows, MEMBERS), jnp.bfloat16),
        in_specs=[VMEM] * len(parts),
        out_specs=VMEM,
        compiler_params=pltpu.CompilerParams(vmem_limit_bytes=4 << 20),
        name="join",
    )(*parts)


def load_kernel(obs, places, out):
    for t in range(BATCHES):
        out[t, :OBS_ROWS] = obs[t]
        held = places[t : t + 1].astype(jnp.float32)
        rows = [held[:, r * EDGE : (r + 1) * EDGE] for r in range(SPAN)]
        rows.append(jnp.zeros((PAD - SPAN, EDGE), jnp.float32))
        out[t, OBS_ROWS:, :EDGE] = jnp.concatenate(rows, axis=0).astype(jnp.bfloat16)
        out[t, OBS_ROWS:, EDGE:] = jnp.zeros((PAD, MEMBERS - EDGE), jnp.bfloat16)


def load(obs, places):
    return pl.pallas_call(
        load_kernel,
        out_shape=jax.ShapeDtypeStruct((BATCHES, OBS_ROWS + PAD, MEMBERS), jnp.bfloat16),
        in_specs=[VMEM, VMEM],
        out_specs=VMEM,
        compiler_params=pltpu.CompilerParams(vmem_limit_bytes=8 << 20),
        name="load",
    )(obs, places)


def relay_kernel(batch, obs, weights, out):
    out[: OBS_ROWS + PAD] = obs[batch]
    out[OBS_ROWS + PAD :] = weights[batch]


def relay(batch, obs, weights):
    return pl.pallas_call(
        functools.partial(relay_kernel, batch),
        out_shape=jax.ShapeDtypeStruct((2 * OBS_ROWS + PAD, MEMBERS), jnp.bfloat16),
        in_specs=[VMEM, VMEM],
        out_specs=VMEM,
        compiler_params=pltpu.CompilerParams(vmem_limit_bytes=8 << 20),
        name="relay",
    )(obs, weights)


def local(ens_state, state_pos, obs_ens, obs_pos, innov_weight, block_rows):
    state = jnp.concatenate(
        [ens_state[0], jnp.pad(state_pos[None, :], ((0, PAD - 1), (0, MEMBERS - SHARD)))], axis=0
    )
    mine = flip(state)
    parts = [mine]
    for mask in (4, 2, 6):
        parts.append(swap_z_flip(state, mask))
    state = join(*parts)
    other = swap_z(state, 1)
    state = pack(state, other)
    pieces = [state]
    for k in range(1, NX):
        pieces.append(swap_x(state, k))

    weight = innov_weight[:, 0]
    weight_left = along_rows(weight, 1)
    weight_right = along_rows(weight, ROWS - 1)
    obs = load(obs_ens[:, 0], obs_pos)
    obs_left = along_rows_flip(obs, 1)
    obs_right = along_rows_flip(obs, ROWS - 1)
    obs_own = flip(obs)
    far0 = relay(0, obs_left, weight_left)
    far0 = along_rows(far0, 1)
    far1 = relay(1, obs_right, weight_right)
    far1 = along_rows(far1, ROWS - 1)

    lists = make_lists(jnp.transpose(block_rows, (0, 2, 1)))
    seen = (obs_own, weight, obs_left, weight_left, obs_right, weight_right)
    early = near(0, lists, (pieces[0], pieces[1], *seen))
    later = near(1, lists, (pieces[2], pieces[3], *seen))
    part2, part3 = far(1, lists, *later, (far0, far1))
    part2 = swap_x(part2, 2)
    part3 = swap_x(part3, 3)
    own, part1 = far(0, lists, *early, (far0, far1))
    part1 = swap_x(part1, 1)
    parts = [part1, part2, part3]
    keep, send = small(sum_x_kernel, (4 * SHARD, 4 * SHARD), own, *parts)
    got = swap_z(send, 1)
    own, *parts = small(sum_z1_kernel, (SHARD,) * 4, keep, got)
    for k, mask in ((1, 4), (0, 2), (2, 6)):
        parts[k] = swap_z(parts[k], mask)
    (total,) = small(sum_z_kernel, (SHARD,), own, *parts)
    return total[None]


def solution(mesh):
    in_specs = (
        P("half", ("rows", "obs"), None),
        P(("rows", "obs")),
        P(None, "half", ("rows", "obs"), None),
        P(None, ("rows", "obs")),
        P(None, "half", ("rows", "obs"), None),
        P(),
    )
    out_specs = P("half", ("rows", "obs"), None)
    return jax.shard_map(local, mesh=mesh, in_specs=in_specs, out_specs=out_specs, check_vma=False)
```

```python
import functools
import math

import jax
import jax.numpy as jnp
from jax import lax
from jax.experimental import pallas as pl
from jax.experimental.pallas import tpu as pltpu
from jax.sharding import PartitionSpec as P


BATCHES = 2
ROWS, HALVES, OBS = 4, 2, 32
NX, NZ = 4, 8
EDGE = 128
SHARD = 64
MEMBERS = 256
RANGE_BLOCKS = 16
SPAN = 4
NAMED = 16
OBS_ROWS = SPAN * EDGE
PAD = 16
Z_ORDER = (0, 4, 2, 6, 1, 5, 3, 7)

TURNS = (0, ROWS - 1, 1, 2)
SPAN_KEYS = BATCHES * RANGE_BLOCKS
DEAD = -1e30
LIVE = math.log2(1.0 / (MEMBERS - 1))
STRETCH = 2.0 * math.sqrt(math.log2(math.e))

VMEM = pl.BlockSpec(memory_space=pltpu.VMEM)


def flip(value):
    return lax.ppermute(value, "half", [(0, 1), (1, 0)])


def along_rows(value, step):
    return lax.ppermute(value, "rows", [(s, (s + step) % ROWS) for s in range(ROWS)])


def along_rows_flip(value, step):
    pairs = [
        (r * HALVES + h, ((r + step) % ROWS) * HALVES + 1 - h)
        for r in range(ROWS)
        for h in range(HALVES)
    ]
    return lax.ppermute(value, ("rows", "half"), pairs)


def swap_z(value, mask):
    pairs = [(z * NX + x, (z ^ mask) * NX + x) for z in range(NZ) for x in range(NX)]
    return lax.ppermute(value, "obs", pairs)


def swap_z_flip(value, mask):
    pairs = [
        (h * OBS + z * NX + x, (1 - h) * OBS + (z ^ mask) * NX + x)
        for h in range(HALVES)
        for z in range(NZ)
        for x in range(NX)
    ]
    return lax.ppermute(value, ("half", "obs"), pairs)


def swap_x(value, mask):
    pairs = [(z * NX + x, z * NX + (x ^ mask)) for z in range(NZ) for x in range(NX)]
    return lax.ppermute(value, "obs", pairs)


def masks_kernel(named, masks, hits):
    row, column = lax.axis_index("rows"), lax.axis_index("obs")
    blocks = lax.broadcasted_iota(jnp.int32, (RANGE_BLOCKS, EDGE), 0) + row * RANGE_BLOCKS
    for chunk in range(ROWS):
        for t in range(BATCHES):
            hit = jnp.zeros((RANGE_BLOCKS, EDGE), jnp.float32)
            for e in range(NAMED):
                picked = named[t, e : e + 1, chunk * EDGE : (chunk + 1) * EDGE]
                hit = jnp.where(picked == blocks, 1.0, hit)
            hits[chunk, t * RANGE_BLOCKS : (t + 1) * RANGE_BLOCKS] = hit
    shift = jnp.bitwise_and(EDGE - column * SPAN, EDGE - 1)
    for k, turn in enumerate(TURNS):
        chunk = hits[jnp.bitwise_and(row + turn, ROWS - 1)]
        rolled = pltpu.roll(chunk, shift, 1)
        for j in range(SPAN):
            wide = jnp.broadcast_to(rolled[:, j : j + 1], (SPAN_KEYS, EDGE))
            masks[k * SPAN_KEYS : (k + 1) * SPAN_KEYS, j * EDGE : (j + 1) * EDGE] = jnp.where(
                wide > 0.5, LIVE, DEAD
            )


def make_masks(named):
    return pl.pallas_call(
        masks_kernel,
        out_shape=jax.ShapeDtypeStruct((len(TURNS) * SPAN_KEYS, SPAN * EDGE), jnp.float32),
        in_specs=[VMEM],
        out_specs=VMEM,
        scratch_shapes=[pltpu.VMEM((ROWS, SPAN_KEYS, EDGE), jnp.float32)],
        compiler_params=pltpu.CompilerParams(vmem_limit_bytes=4 << 20),
        cost_estimate=pl.CostEstimate(flops=4_000_000, transcendentals=0, bytes_accessed=4_000_000),
        name="masks",
    )(named)


def tile_pass(segments, parity, state, spot, acc, places, tiles, masks, base):
    pair = 2 * EDGE
    flat_state = state.reshape((2 * NZ) * SHARD, MEMBERS)
    flat_spot = spot.reshape((2 * NZ) * SHARD, EDGE)

    def make(spans, buffer):
        for u, (key, place, obs) in enumerate(spans):
            for h in range(SPAN // 2):
                here = obs[h * pair : (h + 1) * pair, :]
                products = lax.dot_general(
                    flat_state[...], here, (((1,), (1,)), ((), ())),
                    preferred_element_type=jnp.float32,
                )
                for z in range(NZ):
                    positions = flat_spot[z * EDGE : (z + 1) * EDGE]
                    live = masks[pl.ds(key + 2 * z + parity, 1), h * pair : (h + 1) * pair]
                    for i in range(2):
                        j = 2 * h + i
                        d = positions - places[place + j : place + j + 1, :]
                        part = products[z * EDGE : (z + 1) * EDGE, i * EDGE : (i + 1) * EDGE]
                        damped = part * jnp.exp2(live[:, i * EDGE : (i + 1) * EDGE] - d * d)
                        at = (u * SPAN + j) * EDGE
                        tiles[buffer, z * EDGE : (z + 1) * EDGE, at : at + EDGE] = damped.astype(
                            jnp.bfloat16
                        )

    def add(weights, buffer, first):
        start = 0
        total = None
        for weight in weights:
            depth = weight.shape[0]
            part = jnp.dot(
                tiles[buffer, :, start : start + depth], weight[...],
                preferred_element_type=jnp.float32,
            )
            total = part if total is None else total + part
            start += depth
        total = total.reshape(NZ, EDGE, MEMBERS)
        if not first:
            total = acc[...] + total
        elif base is not None:
            total = base[...] + total
        acc[...] = total

    for n, (spans, weights) in enumerate(segments):
        if n:
            add(segments[n - 1][1], (n - 1) % 2, n == 1)
        make(spans, n % 2)
    last = len(segments) - 1
    add(segments[last][1], last % 2, last == 0)


def spread_places(held, places, start):
    places[start : start + SPAN] = held.astype(jnp.float32)[:SPAN] * STRETCH


def own_place(late):
    column = lax.axis_index("obs")
    my_z = lax.shift_right_logical(column, 2)
    x = jnp.bitwise_xor(jnp.bitwise_and(column, NX - 1), 2 * late)
    return my_z, x


def near_kernel(
    late, masks, p0, p1, oo, wo, ol, wl, orr, wr, state, spot, acc, places, tiles
):
    my_z, x = own_place(late)
    lanes = lax.broadcasted_iota(jnp.int32, (SHARD, EDGE), 1)
    sublanes = lax.broadcasted_iota(jnp.int32, (SHARD, EDGE), 0)
    same = lanes == sublanes
    ones = jnp.ones((EDGE, EDGE), jnp.bfloat16)
    for k, piece in enumerate((p0, p1)):
        half = jnp.bitwise_and(jnp.bitwise_xor(x, k), 1)
        held = piece[NZ * SHARD : NZ * SHARD + PAD, :EDGE].astype(jnp.float32)
        spread = jnp.concatenate(
            [jnp.where(same, held[p : p + 1], 0.0) for p in range(NZ)], axis=0
        ).astype(jnp.bfloat16)
        columns = jnp.dot(spread, ones, preferred_element_type=jnp.float32) * STRETCH
        for p, mask in enumerate(Z_ORDER):
            at = jnp.bitwise_xor(my_z, mask) * 2 + half
            state[at] = piece[p * SHARD : (p + 1) * SHARD, :]
            spot[at] = columns[p * SHARD : (p + 1) * SHARD]
    segments = []
    for k, (o, w) in enumerate(((oo, wo), (ol, wl), (orr, wr))):
        spans = []
        for t in range(BATCHES):
            place = (k * BATCHES + t) * SPAN
            spread_places(o[t, OBS_ROWS : OBS_ROWS + PAD, :EDGE], places, place)
            spans.append((k * SPAN_KEYS + t * RANGE_BLOCKS, place, o.at[t]))
        segments.append((spans, (w.reshape(BATCHES * OBS_ROWS, MEMBERS),)))
    parity = lax.shift_right_logical(x, 1)
    tile_pass(segments, parity, state, spot, acc, places, tiles, masks, None)


SCRATCH = [
    pltpu.VMEM((24, EDGE), jnp.float32),
    pltpu.VMEM((2, NZ * EDGE, BATCHES * SPAN * EDGE), jnp.bfloat16),
]


def near(late, masks, arrays):
    return pl.pallas_call(
        functools.partial(near_kernel, late),
        out_shape=(
            jax.ShapeDtypeStruct((2 * NZ, SHARD, MEMBERS), jnp.bfloat16),
            jax.ShapeDtypeStruct((2 * NZ, SHARD, EDGE), jnp.float32),
            jax.ShapeDtypeStruct((NZ, EDGE, MEMBERS), jnp.float32),
        ),
        in_specs=[VMEM] * 9,
        out_specs=(VMEM,) * 3,
        scratch_shapes=SCRATCH,
        compiler_params=pltpu.CompilerParams(vmem_limit_bytes=20 << 20),
        cost_estimate=pl.CostEstimate(
            flops=2_000_000_000, transcendentals=2_000_000, bytes_accessed=4_000_000
        ),
        name="near_late" if late else "near_early",
    )(masks, *arrays)


def far_kernel(late, masks, state, spot, near_acc, left, right, r0, r1, places, tiles, acc):
    spans, weights = [], []
    for t, both in enumerate((left, right)):
        spread_places(both[OBS_ROWS : OBS_ROWS + PAD, :EDGE], places, t * SPAN)
        spans.append(((len(TURNS) - 1) * SPAN_KEYS + t * RANGE_BLOCKS, t * SPAN, both))
        weights.append(both.at[OBS_ROWS + PAD :])
    _, x = own_place(late)
    parity = lax.shift_right_logical(x, 1)
    segments = [(spans, weights)]
    tile_pass(segments, parity, state, spot, acc, places, tiles, masks, near_acc)
    for k, out in enumerate((r0, r1)):
        half = jnp.bitwise_and(jnp.bitwise_xor(x, k), 1)
        start = pl.multiple_of(half * SHARD, SHARD)
        for z in range(NZ):
            out[z * SHARD : (z + 1) * SHARD] = acc[z, pl.ds(start, SHARD), :].astype(out.dtype)


def far(late, masks, state, spot, acc, arrays):
    rows = NZ * SHARD
    return pl.pallas_call(
        functools.partial(far_kernel, late),
        out_shape=(
            jax.ShapeDtypeStruct((rows, MEMBERS), jnp.bfloat16 if late else jnp.float32),
            jax.ShapeDtypeStruct((rows, MEMBERS), jnp.bfloat16),
        ),
        in_specs=[VMEM] * 6,
        out_specs=(VMEM, VMEM),
        scratch_shapes=SCRATCH + [pltpu.VMEM((NZ, EDGE, MEMBERS), jnp.float32)],
        compiler_params=pltpu.CompilerParams(vmem_limit_bytes=20 << 20),
        cost_estimate=pl.CostEstimate(
            flops=500_000_000, transcendentals=500_000, bytes_accessed=4_000_000
        ),
        name="far_late" if late else "far_early",
    )(masks, state, spot, acc, *arrays)


def sum_x_kernel(own, x1, x2, x3, keep, send):
    my_z = lax.shift_right_logical(lax.axis_index("obs"), 2)
    for mask in range(NZ):
        rows = pl.ds(pl.multiple_of(jnp.bitwise_xor(my_z, mask) * SHARD, SHARD), SHARD)
        total = own[rows, :]
        for ref in (x1, x2, x3):
            total += ref[rows, :].astype(jnp.float32)
        out, k = (send if mask & 1 else keep), mask // 2
        out[k * SHARD : (k + 1) * SHARD] = total


def sum_z1_kernel(keep, got, own, z2, z4, z6):
    for k, out in enumerate((own, z2, z4, z6)):
        rows = slice(k * SHARD, (k + 1) * SHARD)
        out[...] = keep[rows] + got[rows]


def sum_z_kernel(own, z2, z4, z6, out):
    out[...] = own[...] + z2[...] + z4[...] + z6[...]


def small(body, out_rows, *arrays):
    return pl.pallas_call(
        body,
        out_shape=tuple(jax.ShapeDtypeStruct((r, MEMBERS), jnp.float32) for r in out_rows),
        in_specs=[VMEM] * len(arrays),
        out_specs=(VMEM,) * len(out_rows),
        compiler_params=pltpu.CompilerParams(vmem_limit_bytes=6 << 20),
    )(*arrays)


def pack_kernel(a, b, out):
    held = SHARD + PAD
    places = []
    for p in range(NZ):
        ref, q = (a, p) if p < NZ // 2 else (b, p - NZ // 2)
        out[p * SHARD : (p + 1) * SHARD] = ref[q * held : q * held + SHARD]
        places.append(ref[q * held + SHARD : (q + 1) * held].astype(jnp.float32)[:1])
    places.append(jnp.zeros((PAD - NZ, MEMBERS), jnp.float32))
    out[NZ * SHARD :] = jnp.concatenate(places, axis=0).astype(jnp.bfloat16)


def pack(a, b):
    return pl.pallas_call(
        pack_kernel,
        out_shape=jax.ShapeDtypeStruct((NZ * SHARD + PAD, MEMBERS), jnp.bfloat16),
        in_specs=[VMEM, VMEM],
        out_specs=VMEM,
        compiler_params=pltpu.CompilerParams(vmem_limit_bytes=4 << 20),
        name="pack",
    )(a, b)


def join_kernel(*refs):
    out = refs[-1]
    start = 0
    for ref in refs[:-1]:
        out[start : start + ref.shape[0]] = ref[...]
        start += ref.shape[0]


def join(*parts):
    rows = sum(part.shape[0] for part in parts)
    return pl.pallas_call(
        join_kernel,
        out_shape=jax.ShapeDtypeStruct((rows, MEMBERS), jnp.bfloat16),
        in_specs=[VMEM] * len(parts),
        out_specs=VMEM,
        compiler_params=pltpu.CompilerParams(vmem_limit_bytes=4 << 20),
        name="join",
    )(*parts)


def load_kernel(obs, places, out):
    for t in range(BATCHES):
        out[t, :OBS_ROWS] = obs[t]
        held = places[t : t + 1].astype(jnp.float32)
        rows = [held[:, r * EDGE : (r + 1) * EDGE] for r in range(SPAN)]
        rows.append(jnp.zeros((PAD - SPAN, EDGE), jnp.float32))
        out[t, OBS_ROWS:, :EDGE] = jnp.concatenate(rows, axis=0).astype(jnp.bfloat16)
        out[t, OBS_ROWS:, EDGE:] = jnp.zeros((PAD, MEMBERS - EDGE), jnp.bfloat16)


def load(obs, places):
    return pl.pallas_call(
        load_kernel,
        out_shape=jax.ShapeDtypeStruct((BATCHES, OBS_ROWS + PAD, MEMBERS), jnp.bfloat16),
        in_specs=[VMEM, VMEM],
        out_specs=VMEM,
        compiler_params=pltpu.CompilerParams(vmem_limit_bytes=8 << 20),
        name="load",
    )(obs, places)


def relay_kernel(batch, obs, weights, out):
    out[: OBS_ROWS + PAD] = obs[batch]
    out[OBS_ROWS + PAD :] = weights[batch]


def relay(batch, obs, weights):
    return pl.pallas_call(
        functools.partial(relay_kernel, batch),
        out_shape=jax.ShapeDtypeStruct((2 * OBS_ROWS + PAD, MEMBERS), jnp.bfloat16),
        in_specs=[VMEM, VMEM],
        out_specs=VMEM,
        compiler_params=pltpu.CompilerParams(vmem_limit_bytes=8 << 20),
        name="relay",
    )(obs, weights)


def local(ens_state, state_pos, obs_ens, obs_pos, innov_weight, block_rows):
    state = jnp.concatenate(
        [ens_state[0], jnp.pad(state_pos[None, :], ((0, PAD - 1), (0, MEMBERS - SHARD)))], axis=0
    )
    mine = flip(state)
    parts = [mine]
    for mask in (4, 2, 6):
        parts.append(swap_z_flip(state, mask))
    state = join(*parts)
    other = swap_z(state, 1)
    state = pack(state, other)
    pieces = [state]
    for k in range(1, NX):
        pieces.append(swap_x(state, k))

    weight = innov_weight[:, 0]
    weight_left = along_rows(weight, 1)
    weight_right = along_rows(weight, ROWS - 1)
    obs = load(obs_ens[:, 0], obs_pos)
    obs_left = along_rows_flip(obs, 1)
    obs_right = along_rows_flip(obs, ROWS - 1)
    obs_own = flip(obs)
    far0 = relay(0, obs_left, weight_left)
    far0 = along_rows(far0, 1)
    far1 = relay(1, obs_right, weight_right)
    far1 = along_rows(far1, ROWS - 1)

    masks = make_masks(jnp.transpose(block_rows, (0, 2, 1)))
    seen = (obs_own, weight, obs_left, weight_left, obs_right, weight_right)
    early = near(0, masks, (pieces[0], pieces[1], *seen))
    later = near(1, masks, (pieces[2], pieces[3], *seen))
    part2, part3 = far(1, masks, *later, (far0, far1))
    part2 = swap_x(part2, 2)
    part3 = swap_x(part3, 3)
    own, part1 = far(0, masks, *early, (far0, far1))
    part1 = swap_x(part1, 1)
    parts = [part1, part2, part3]
    keep, send = small(sum_x_kernel, (4 * SHARD, 4 * SHARD), own, *parts)
    got = swap_z(send, 1)
    own, *parts = small(sum_z1_kernel, (SHARD,) * 4, keep, got)
    for k, mask in ((1, 4), (0, 2), (2, 6)):
        parts[k] = swap_z(parts[k], mask)
    (total,) = small(sum_z_kernel, (SHARD,), own, *parts)
    return total[None]


def solution(mesh):
    in_specs = (
        P("half", ("rows", "obs"), None),
        P(("rows", "obs")),
        P(None, "half", ("rows", "obs"), None),
        P(None, ("rows", "obs")),
        P(None, "half", ("rows", "obs"), None),
        P(),
    )
    out_specs = P("half", ("rows", "obs"), None)
    return jax.shard_map(local, mesh=mesh, in_specs=in_specs, out_specs=out_specs, check_vma=False)
```

```python
import functools
import math

import jax
import jax.numpy as jnp
from jax import lax
from jax.experimental import pallas as pl
from jax.experimental.pallas import tpu as pltpu
from jax.sharding import PartitionSpec as P


BATCHES = 2
ROWS, HALVES, OBS = 4, 2, 32
NX, NZ = 4, 8
EDGE = 128
SHARD = 64
MEMBERS = 256
RANGE_BLOCKS = 16
SPAN = 4
NAMED = 16
OBS_ROWS = SPAN * EDGE
PAD = 16
Z_ORDER = (0, 4, 2, 6, 1, 5, 3, 7)

TURNS = (0, ROWS - 1, 1, 2)
SPAN_KEYS = BATCHES * RANGE_BLOCKS
DEAD = -1e30
LIVE = math.log2(1.0 / (MEMBERS - 1))
STRETCH = 2.0 * math.sqrt(math.log2(math.e))

VMEM = pl.BlockSpec(memory_space=pltpu.VMEM)


def flip(value):
    return lax.ppermute(value, "half", [(0, 1), (1, 0)])


def along_rows(value, step):
    return lax.ppermute(value, "rows", [(s, (s + step) % ROWS) for s in range(ROWS)])


def along_rows_flip(value, step):
    pairs = [
        (r * HALVES + h, ((r + step) % ROWS) * HALVES + 1 - h)
        for r in range(ROWS)
        for h in range(HALVES)
    ]
    return lax.ppermute(value, ("rows", "half"), pairs)


def swap_z(value, mask):
    pairs = [(z * NX + x, (z ^ mask) * NX + x) for z in range(NZ) for x in range(NX)]
    return lax.ppermute(value, "obs", pairs)


def swap_z_flip(value, mask):
    pairs = [
        (h * OBS + z * NX + x, (1 - h) * OBS + (z ^ mask) * NX + x)
        for h in range(HALVES)
        for z in range(NZ)
        for x in range(NX)
    ]
    return lax.ppermute(value, ("half", "obs"), pairs)


def swap_x(value, mask):
    pairs = [(z * NX + x, z * NX + (x ^ mask)) for z in range(NZ) for x in range(NX)]
    return lax.ppermute(value, "obs", pairs)


def masks_kernel(named, masks, hits):
    row, column = lax.axis_index("rows"), lax.axis_index("obs")
    blocks = lax.broadcasted_iota(jnp.int32, (RANGE_BLOCKS, EDGE), 0) + row * RANGE_BLOCKS
    for chunk in range(ROWS):
        for t in range(BATCHES):
            hit = jnp.zeros((RANGE_BLOCKS, EDGE), jnp.float32)
            for e in range(NAMED):
                picked = named[t, e : e + 1, chunk * EDGE : (chunk + 1) * EDGE]
                hit = jnp.where(picked == blocks, 1.0, hit)
            hits[chunk, t * RANGE_BLOCKS : (t + 1) * RANGE_BLOCKS] = hit
    shift = jnp.bitwise_and(EDGE - column * SPAN, EDGE - 1)
    for k, turn in enumerate(TURNS):
        chunk = hits[jnp.bitwise_and(row + turn, ROWS - 1)]
        rolled = pltpu.roll(chunk, shift, 1)
        for j in range(SPAN):
            wide = jnp.broadcast_to(rolled[:, j : j + 1], (SPAN_KEYS, EDGE))
            masks[k * SPAN_KEYS : (k + 1) * SPAN_KEYS, j * EDGE : (j + 1) * EDGE] = jnp.where(
                wide > 0.5, LIVE, DEAD
            )


def make_masks(named):
    return pl.pallas_call(
        masks_kernel,
        out_shape=jax.ShapeDtypeStruct((len(TURNS) * SPAN_KEYS, SPAN * EDGE), jnp.float32),
        in_specs=[VMEM],
        out_specs=VMEM,
        scratch_shapes=[pltpu.VMEM((ROWS, SPAN_KEYS, EDGE), jnp.float32)],
        compiler_params=pltpu.CompilerParams(vmem_limit_bytes=4 << 20),
        cost_estimate=pl.CostEstimate(flops=4_000_000, transcendentals=0, bytes_accessed=4_000_000),
        name="masks",
    )(named)


def tile_pass(segments, parity, state, spot, acc, places, tiles, masks, base):
    pair = 2 * EDGE
    flat_state = state.reshape((2 * NZ) * SHARD, MEMBERS)
    flat_spot = spot.reshape((2 * NZ) * SHARD, EDGE)

    def make(spans, buffer):
        for u, (key, place, obs) in enumerate(spans):
            for h in range(SPAN // 2):
                here = obs[h * pair : (h + 1) * pair, :]
                products = lax.dot_general(
                    flat_state[...], here, (((1,), (1,)), ((), ())),
                    preferred_element_type=jnp.float32,
                )
                for z in range(NZ):
                    positions = flat_spot[z * EDGE : (z + 1) * EDGE]
                    live = masks[pl.ds(key + 2 * z + parity, 1), h * pair : (h + 1) * pair]
                    for i in range(2):
                        j = 2 * h + i
                        d = positions - places[place + j : place + j + 1, :]
                        part = products[z * EDGE : (z + 1) * EDGE, i * EDGE : (i + 1) * EDGE]
                        damped = part * jnp.exp2(live[:, i * EDGE : (i + 1) * EDGE] - d * d)
                        at = (u * SPAN + j) * EDGE
                        tiles[buffer, z * EDGE : (z + 1) * EDGE, at : at + EDGE] = damped.astype(
                            jnp.bfloat16
                        )

    def add(weights, buffer, first):
        start = 0
        total = None
        for weight in weights:
            depth = weight.shape[0]
            part = jnp.dot(
                tiles[buffer, :, start : start + depth], weight[...],
                preferred_element_type=jnp.float32,
            )
            total = part if total is None else total + part
            start += depth
        total = total.reshape(NZ, EDGE, MEMBERS)
        if not first:
            total = acc[...] + total
        elif base is not None:
            total = base[...] + total
        acc[...] = total

    for n, (spans, weights) in enumerate(segments):
        if n:
            add(segments[n - 1][1], (n - 1) % 2, n == 1)
        make(spans, n % 2)
    last = len(segments) - 1
    add(segments[last][1], last % 2, last == 0)


def spread_places(held, places, start):
    places[start : start + SPAN] = held.astype(jnp.float32)[:SPAN] * STRETCH


def own_place(late):
    column = lax.axis_index("obs")
    my_z = lax.shift_right_logical(column, 2)
    x = jnp.bitwise_xor(jnp.bitwise_and(column, NX - 1), 2 * late)
    return my_z, x


def near_kernel(
    late, masks, p0, p1, oo, wo, ol, wl, orr, wr, state, spot, acc, places, tiles
):
    my_z, x = own_place(late)
    lanes = lax.broadcasted_iota(jnp.int32, (SHARD, EDGE), 1)
    sublanes = lax.broadcasted_iota(jnp.int32, (SHARD, EDGE), 0)
    same = lanes == sublanes
    ones = jnp.ones((EDGE, EDGE), jnp.bfloat16)
    for k, piece in enumerate((p0, p1)):
        half = jnp.bitwise_and(jnp.bitwise_xor(x, k), 1)
        held = piece[NZ * SHARD : NZ * SHARD + PAD, :EDGE].astype(jnp.float32)
        spread = jnp.concatenate(
            [jnp.where(same, held[p : p + 1], 0.0) for p in range(NZ)], axis=0
        ).astype(jnp.bfloat16)
        columns = jnp.dot(spread, ones, preferred_element_type=jnp.float32) * STRETCH
        for p, mask in enumerate(Z_ORDER):
            at = jnp.bitwise_xor(my_z, mask) * 2 + half
            state[at] = piece[p * SHARD : (p + 1) * SHARD, :]
            spot[at] = columns[p * SHARD : (p + 1) * SHARD]
    segments = []
    for k, (o, w) in enumerate(((oo, wo), (ol, wl), (orr, wr))):
        spans = []
        for t in range(BATCHES):
            place = (k * BATCHES + t) * SPAN
            spread_places(o[t, OBS_ROWS : OBS_ROWS + PAD, :EDGE], places, place)
            spans.append((k * SPAN_KEYS + t * RANGE_BLOCKS, place, o.at[t]))
        segments.append((spans, (w.reshape(BATCHES * OBS_ROWS, MEMBERS),)))
    parity = lax.shift_right_logical(x, 1)
    tile_pass(segments, parity, state, spot, acc, places, tiles, masks, None)


SCRATCH = [
    pltpu.VMEM((24, EDGE), jnp.float32),
    pltpu.VMEM((2, NZ * EDGE, BATCHES * SPAN * EDGE), jnp.bfloat16),
]


def near(late, masks, arrays):
    return pl.pallas_call(
        functools.partial(near_kernel, late),
        out_shape=(
            jax.ShapeDtypeStruct((2 * NZ, SHARD, MEMBERS), jnp.bfloat16),
            jax.ShapeDtypeStruct((2 * NZ, SHARD, EDGE), jnp.float32),
            jax.ShapeDtypeStruct((NZ, EDGE, MEMBERS), jnp.float32),
        ),
        in_specs=[VMEM] * 9,
        out_specs=(VMEM,) * 3,
        scratch_shapes=SCRATCH,
        compiler_params=pltpu.CompilerParams(vmem_limit_bytes=20 << 20),
        cost_estimate=pl.CostEstimate(
            flops=2_000_000_000, transcendentals=2_000_000, bytes_accessed=4_000_000
        ),
        name="near_late" if late else "near_early",
    )(masks, *arrays)


def far_kernel(late, masks, state, spot, near_acc, left, right, r0, r1, places, tiles, acc):
    spans, weights = [], []
    for t, both in enumerate((left, right)):
        spread_places(both[OBS_ROWS : OBS_ROWS + PAD, :EDGE], places, t * SPAN)
        spans.append(((len(TURNS) - 1) * SPAN_KEYS + t * RANGE_BLOCKS, t * SPAN, both))
        weights.append(both.at[OBS_ROWS + PAD :])
    _, x = own_place(late)
    parity = lax.shift_right_logical(x, 1)
    segments = [(spans, weights)]
    tile_pass(segments, parity, state, spot, acc, places, tiles, masks, near_acc)
    for k, out in enumerate((r0, r1)):
        half = jnp.bitwise_and(jnp.bitwise_xor(x, k), 1)
        start = pl.multiple_of(half * SHARD, SHARD)
        for z in range(NZ):
            out[z * SHARD : (z + 1) * SHARD] = acc[z, pl.ds(start, SHARD), :].astype(out.dtype)


def far(late, masks, state, spot, acc, arrays):
    rows = NZ * SHARD
    return pl.pallas_call(
        functools.partial(far_kernel, late),
        out_shape=(
            jax.ShapeDtypeStruct((rows, MEMBERS), jnp.bfloat16 if late else jnp.float32),
            jax.ShapeDtypeStruct((rows, MEMBERS), jnp.bfloat16),
        ),
        in_specs=[VMEM] * 6,
        out_specs=(VMEM, VMEM),
        scratch_shapes=SCRATCH + [pltpu.VMEM((NZ, EDGE, MEMBERS), jnp.float32)],
        compiler_params=pltpu.CompilerParams(vmem_limit_bytes=20 << 20),
        cost_estimate=pl.CostEstimate(
            flops=500_000_000, transcendentals=500_000, bytes_accessed=4_000_000
        ),
        name="far_late" if late else "far_early",
    )(masks, state, spot, acc, *arrays)


def sum_x_kernel(own, x1, x2, x3, keep, send):
    my_z = lax.shift_right_logical(lax.axis_index("obs"), 2)
    for mask in range(NZ):
        rows = pl.ds(pl.multiple_of(jnp.bitwise_xor(my_z, mask) * SHARD, SHARD), SHARD)
        total = own[rows, :]
        for ref in (x1, x2, x3):
            total += ref[rows, :].astype(jnp.float32)
        out, k = (send if mask & 1 else keep), mask // 2
        out[k * SHARD : (k + 1) * SHARD] = total.astype(out.dtype)


def sum_z1_kernel(keep, got, own, z2, z4, z6):
    for k, out in enumerate((own, z2, z4, z6)):
        rows = slice(k * SHARD, (k + 1) * SHARD)
        out[...] = (keep[rows] + got[rows].astype(jnp.float32)).astype(out.dtype)


def sum_z_kernel(own, z2, z4, z6, out):
    total = own[...]
    for ref in (z2, z4, z6):
        total += ref[...].astype(jnp.float32)
    out[...] = total


def small(body, out_rows, *arrays):
    return pl.pallas_call(
        body,
        out_shape=tuple(
            jax.ShapeDtypeStruct((rows, MEMBERS), jnp.bfloat16 if n else jnp.float32)
            for n, rows in enumerate(out_rows)
        ),
        in_specs=[VMEM] * len(arrays),
        out_specs=(VMEM,) * len(out_rows),
        compiler_params=pltpu.CompilerParams(vmem_limit_bytes=6 << 20),
    )(*arrays)


def pack_kernel(a, b, out):
    held = SHARD + PAD
    places = []
    for p in range(NZ):
        ref, q = (a, p) if p < NZ // 2 else (b, p - NZ // 2)
        out[p * SHARD : (p + 1) * SHARD] = ref[q * held : q * held + SHARD]
        places.append(ref[q * held + SHARD : (q + 1) * held].astype(jnp.float32)[:1])
    places.append(jnp.zeros((PAD - NZ, MEMBERS), jnp.float32))
    out[NZ * SHARD :] = jnp.concatenate(places, axis=0).astype(jnp.bfloat16)


def pack(a, b):
    return pl.pallas_call(
        pack_kernel,
        out_shape=jax.ShapeDtypeStruct((NZ * SHARD + PAD, MEMBERS), jnp.bfloat16),
        in_specs=[VMEM, VMEM],
        out_specs=VMEM,
        compiler_params=pltpu.CompilerParams(vmem_limit_bytes=4 << 20),
        name="pack",
    )(a, b)


def join_kernel(*refs):
    out = refs[-1]
    start = 0
    for ref in refs[:-1]:
        out[start : start + ref.shape[0]] = ref[...]
        start += ref.shape[0]


def join(*parts):
    rows = sum(part.shape[0] for part in parts)
    return pl.pallas_call(
        join_kernel,
        out_shape=jax.ShapeDtypeStruct((rows, MEMBERS), jnp.bfloat16),
        in_specs=[VMEM] * len(parts),
        out_specs=VMEM,
        compiler_params=pltpu.CompilerParams(vmem_limit_bytes=4 << 20),
        name="join",
    )(*parts)


def load_kernel(
    state_in, state_pos, obs_in, obs_pos, state, obs, state_places, obs_places, sems
):
    copies = [
        pltpu.make_async_copy(state_pos, state_places, sems.at[0]),
        pltpu.make_async_copy(state_in.at[0], state.at[:SHARD], sems.at[1]),
        pltpu.make_async_copy(obs_pos, obs_places, sems.at[2]),
        pltpu.make_async_copy(obs_in.at[0, 0], obs.at[0, :OBS_ROWS], sems.at[3]),
        pltpu.make_async_copy(obs_in.at[1, 0], obs.at[1, :OBS_ROWS], sems.at[4]),
    ]
    for copy in copies:
        copy.start()
    copies[0].wait()
    held = state_places[...].astype(jnp.float32)
    row = jnp.concatenate([held, jnp.zeros((1, MEMBERS - SHARD), jnp.float32)], axis=1)
    rows = jnp.concatenate([row, jnp.zeros((PAD - 1, MEMBERS), jnp.float32)], axis=0)
    state[SHARD:] = rows.astype(jnp.bfloat16)
    copies[2].wait()
    for t in range(BATCHES):
        held = obs_places[t : t + 1].astype(jnp.float32)
        rows = [held[:, r * EDGE : (r + 1) * EDGE] for r in range(SPAN)]
        rows.append(jnp.zeros((PAD - SPAN, EDGE), jnp.float32))
        obs[t, OBS_ROWS:, :EDGE] = jnp.concatenate(rows, axis=0).astype(jnp.bfloat16)
        obs[t, OBS_ROWS:, EDGE:] = jnp.zeros((PAD, MEMBERS - EDGE), jnp.bfloat16)
    for k in (1, 3, 4):
        copies[k].wait()


def load(state, state_pos, obs, obs_pos):
    return pl.pallas_call(
        load_kernel,
        out_shape=(
            jax.ShapeDtypeStruct((SHARD + PAD, MEMBERS), jnp.bfloat16),
            jax.ShapeDtypeStruct((BATCHES, OBS_ROWS + PAD, MEMBERS), jnp.bfloat16),
        ),
        in_specs=[pl.BlockSpec(memory_space=pltpu.HBM)] * 4,
        out_specs=(VMEM, VMEM),
        scratch_shapes=[
            pltpu.VMEM((1, SHARD), jnp.bfloat16),
            pltpu.VMEM((BATCHES, SPAN * EDGE), jnp.bfloat16),
            pltpu.SemaphoreType.DMA((5,)),
        ],
        compiler_params=pltpu.CompilerParams(vmem_limit_bytes=8 << 20),
        name="load",
    )(state, state_pos, obs, obs_pos)


def relay_kernel(batch, obs, weights, out):
    out[: OBS_ROWS + PAD] = obs[batch]
    out[OBS_ROWS + PAD :] = weights[batch]


def relay(batch, obs, weights):
    return pl.pallas_call(
        functools.partial(relay_kernel, batch),
        out_shape=jax.ShapeDtypeStruct((2 * OBS_ROWS + PAD, MEMBERS), jnp.bfloat16),
        in_specs=[VMEM, VMEM],
        out_specs=VMEM,
        compiler_params=pltpu.CompilerParams(vmem_limit_bytes=8 << 20),
        name="relay",
    )(obs, weights)


def local(ens_state, state_pos, obs_ens, obs_pos, innov_weight, block_rows):
    state, obs = load(ens_state, state_pos[None], obs_ens, obs_pos)
    mine = flip(state)
    parts = [mine]
    for mask in (4, 2, 6):
        parts.append(swap_z_flip(state, mask))
    state = join(*parts)
    other = swap_z(state, 1)
    state = pack(state, other)
    pieces = [state]
    for k in range(1, NX):
        pieces.append(swap_x(state, k))

    weight = innov_weight[:, 0]
    weight_left = along_rows(weight, 1)
    weight_right = along_rows(weight, ROWS - 1)
    obs_left = along_rows_flip(obs, 1)
    obs_right = along_rows_flip(obs, ROWS - 1)
    obs_own = flip(obs)
    far0 = relay(0, obs_left, weight_left)
    far0 = along_rows(far0, 1)
    far1 = relay(1, obs_right, weight_right)
    far1 = along_rows(far1, ROWS - 1)

    masks = make_masks(jnp.transpose(block_rows, (0, 2, 1)))
    seen = (obs_own, weight, obs_left, weight_left, obs_right, weight_right)
    early = near(0, masks, (pieces[0], pieces[1], *seen))
    later = near(1, masks, (pieces[2], pieces[3], *seen))
    part2, part3 = far(1, masks, *later, (far0, far1))
    part2 = swap_x(part2, 2)
    part3 = swap_x(part3, 3)
    own, part1 = far(0, masks, *early, (far0, far1))
    part1 = swap_x(part1, 1)
    parts = [part1, part2, part3]
    keep, send = small(sum_x_kernel, (4 * SHARD, 4 * SHARD), own, *parts)
    got = swap_z(send, 1)
    own, *parts = small(sum_z1_kernel, (SHARD,) * 4, keep, got)
    for k, mask in ((1, 4), (0, 2), (2, 6)):
        parts[k] = swap_z(parts[k], mask)
    (total,) = small(sum_z_kernel, (SHARD,), own, *parts)
    return total[None]


def solution(mesh):
    in_specs = (
        P("half", ("rows", "obs"), None),
        P(("rows", "obs")),
        P(None, "half", ("rows", "obs"), None),
        P(None, ("rows", "obs")),
        P(None, "half", ("rows", "obs"), None),
        P(),
    )
    out_specs = P("half", ("rows", "obs"), None)
    return jax.shard_map(local, mesh=mesh, in_specs=in_specs, out_specs=out_specs, check_vma=False)
```

```python
import functools
import math

import jax
import jax.numpy as jnp
from jax import lax
from jax.experimental import pallas as pl
from jax.experimental.pallas import tpu as pltpu
from jax.sharding import PartitionSpec as P


BATCHES = 2
ROWS, HALVES, OBS = 4, 2, 32
NX, NZ = 4, 8
EDGE = 128
SHARD = 64
MEMBERS = 256
RANGE_BLOCKS = 16
SPAN = 4
NAMED = 16
OBS_ROWS = SPAN * EDGE
PAD = 16
Z_ORDER = (0, 1, 4, 5, 2, 3, 6, 7)

TURNS = (0, ROWS - 1, 1, 2)
SPAN_KEYS = BATCHES * RANGE_BLOCKS
DEAD = -1e30
LIVE = math.log2(1.0 / (MEMBERS - 1))
STRETCH = 2.0 * math.sqrt(math.log2(math.e))

VMEM = pl.BlockSpec(memory_space=pltpu.VMEM)


def flip(value):
    return lax.ppermute(value, "half", [(0, 1), (1, 0)])


def along_rows(value, step):
    return lax.ppermute(value, "rows", [(s, (s + step) % ROWS) for s in range(ROWS)])


def along_rows_flip(value, step):
    pairs = [
        (r * HALVES + h, ((r + step) % ROWS) * HALVES + 1 - h)
        for r in range(ROWS)
        for h in range(HALVES)
    ]
    return lax.ppermute(value, ("rows", "half"), pairs)


def swap_z(value, mask):
    pairs = [(z * NX + x, (z ^ mask) * NX + x) for z in range(NZ) for x in range(NX)]
    return lax.ppermute(value, "obs", pairs)


def swap_z_flip(value, mask):
    pairs = [
        (h * OBS + z * NX + x, (1 - h) * OBS + (z ^ mask) * NX + x)
        for h in range(HALVES)
        for z in range(NZ)
        for x in range(NX)
    ]
    return lax.ppermute(value, ("half", "obs"), pairs)


def swap_x(value, mask):
    pairs = [(z * NX + x, z * NX + (x ^ mask)) for z in range(NZ) for x in range(NX)]
    return lax.ppermute(value, "obs", pairs)


def masks_kernel(named, masks, hits):
    row, column = lax.axis_index("rows"), lax.axis_index("obs")
    blocks = lax.broadcasted_iota(jnp.int32, (RANGE_BLOCKS, EDGE), 0) + row * RANGE_BLOCKS
    for chunk in range(ROWS):
        for t in range(BATCHES):
            hit = jnp.zeros((RANGE_BLOCKS, EDGE), jnp.float32)
            for e in range(NAMED):
                picked = named[t, e : e + 1, chunk * EDGE : (chunk + 1) * EDGE]
                hit = jnp.where(picked == blocks, 1.0, hit)
            hits[chunk, t * RANGE_BLOCKS : (t + 1) * RANGE_BLOCKS] = hit
    shift = jnp.bitwise_and(EDGE - column * SPAN, EDGE - 1)
    for k, turn in enumerate(TURNS):
        chunk = hits[jnp.bitwise_and(row + turn, ROWS - 1)]
        rolled = pltpu.roll(chunk, shift, 1)
        for j in range(SPAN):
            wide = jnp.broadcast_to(rolled[:, j : j + 1], (SPAN_KEYS, EDGE))
            masks[k * SPAN_KEYS : (k + 1) * SPAN_KEYS, j * EDGE : (j + 1) * EDGE] = jnp.where(
                wide > 0.5, LIVE, DEAD
            )


def make_masks(named):
    return pl.pallas_call(
        masks_kernel,
        out_shape=jax.ShapeDtypeStruct((len(TURNS) * SPAN_KEYS, SPAN * EDGE), jnp.float32),
        in_specs=[VMEM],
        out_specs=VMEM,
        scratch_shapes=[pltpu.VMEM((ROWS, SPAN_KEYS, EDGE), jnp.float32)],
        compiler_params=pltpu.CompilerParams(vmem_limit_bytes=4 << 20),
        cost_estimate=pl.CostEstimate(flops=4_000_000, transcendentals=0, bytes_accessed=4_000_000),
        name="masks",
    )(named)


def tile_pass(segments, parity, state, spot, acc, places, tiles, masks, base):
    pair = 2 * EDGE
    flat_state = state.reshape((2 * NZ) * SHARD, MEMBERS)
    flat_spot = spot.reshape((2 * NZ) * SHARD, EDGE)

    def make(spans, buffer):
        for u, (key, place, obs) in enumerate(spans):
            for h in range(SPAN // 2):
                here = obs[h * pair : (h + 1) * pair, :]
                products = lax.dot_general(
                    flat_state[...], here, (((1,), (1,)), ((), ())),
                    preferred_element_type=jnp.float32,
                )
                for z in range(NZ):
                    positions = flat_spot[z * EDGE : (z + 1) * EDGE]
                    live = masks[pl.ds(key + 2 * z + parity, 1), h * pair : (h + 1) * pair]
                    for i in range(2):
                        j = 2 * h + i
                        d = positions - places[place + j : place + j + 1, :]
                        part = products[z * EDGE : (z + 1) * EDGE, i * EDGE : (i + 1) * EDGE]
                        damped = part * jnp.exp2(live[:, i * EDGE : (i + 1) * EDGE] - d * d)
                        at = (u * SPAN + j) * EDGE
                        tiles[buffer, z * EDGE : (z + 1) * EDGE, at : at + EDGE] = damped.astype(
                            jnp.bfloat16
                        )

    def add(weights, buffer, first):
        start = 0
        total = None
        for weight in weights:
            depth = weight.shape[0]
            part = jnp.dot(
                tiles[buffer, :, start : start + depth], weight[...],
                preferred_element_type=jnp.float32,
            )
            total = part if total is None else total + part
            start += depth
        total = total.reshape(NZ, EDGE, MEMBERS)
        if not first:
            total = acc[...] + total
        elif base is not None:
            total = base[...] + total
        acc[...] = total

    for n, (spans, weights) in enumerate(segments):
        if n:
            add(segments[n - 1][1], (n - 1) % 2, n == 1)
        make(spans, n % 2)
    last = len(segments) - 1
    add(segments[last][1], last % 2, last == 0)


def spread_places(held, places, start):
    places[start : start + SPAN] = held.astype(jnp.float32)[:SPAN] * STRETCH


def own_place(late):
    column = lax.axis_index("obs")
    my_z = lax.shift_right_logical(column, 2)
    x = jnp.bitwise_xor(jnp.bitwise_and(column, NX - 1), 2 * late)
    return my_z, x


def near_kernel(
    late, masks, p0, p1, oo, wo, ol, wl, orr, wr, state, spot, acc, places, tiles
):
    my_z, x = own_place(late)
    lanes = lax.broadcasted_iota(jnp.int32, (SHARD, EDGE), 1)
    sublanes = lax.broadcasted_iota(jnp.int32, (SHARD, EDGE), 0)
    same = lanes == sublanes
    ones = jnp.ones((EDGE, EDGE), jnp.bfloat16)
    for k, piece in enumerate((p0, p1)):
        half = jnp.bitwise_and(jnp.bitwise_xor(x, k), 1)
        held = piece[NZ * SHARD : NZ * SHARD + PAD, :EDGE].astype(jnp.float32)
        spread = jnp.concatenate(
            [jnp.where(same, held[p : p + 1], 0.0) for p in range(NZ)], axis=0
        ).astype(jnp.bfloat16)
        columns = jnp.dot(spread, ones, preferred_element_type=jnp.float32) * STRETCH
        for p, mask in enumerate(Z_ORDER):
            at = jnp.bitwise_xor(my_z, mask) * 2 + half
            state[at] = piece[p * SHARD : (p + 1) * SHARD, :]
            spot[at] = columns[p * SHARD : (p + 1) * SHARD]
    segments = []
    for k, (o, w) in enumerate(((oo, wo), (ol, wl), (orr, wr))):
        spans = []
        for t in range(BATCHES):
            place = (k * BATCHES + t) * SPAN
            spread_places(o[t, OBS_ROWS : OBS_ROWS + PAD, :EDGE], places, place)
            spans.append((k * SPAN_KEYS + t * RANGE_BLOCKS, place, o.at[t]))
        segments.append((spans, (w.reshape(BATCHES * OBS_ROWS, MEMBERS),)))
    parity = lax.shift_right_logical(x, 1)
    tile_pass(segments, parity, state, spot, acc, places, tiles, masks, None)


SCRATCH = [
    pltpu.VMEM((24, EDGE), jnp.float32),
    pltpu.VMEM((2, NZ * EDGE, BATCHES * SPAN * EDGE), jnp.bfloat16),
]


def near(late, masks, arrays):
    return pl.pallas_call(
        functools.partial(near_kernel, late),
        out_shape=(
            jax.ShapeDtypeStruct((2 * NZ, SHARD, MEMBERS), jnp.bfloat16),
            jax.ShapeDtypeStruct((2 * NZ, SHARD, EDGE), jnp.float32),
            jax.ShapeDtypeStruct((NZ, EDGE, MEMBERS), jnp.float32),
        ),
        in_specs=[VMEM] * 9,
        out_specs=(VMEM,) * 3,
        scratch_shapes=SCRATCH,
        compiler_params=pltpu.CompilerParams(vmem_limit_bytes=20 << 20),
        cost_estimate=pl.CostEstimate(
            flops=2_000_000_000, transcendentals=2_000_000, bytes_accessed=4_000_000
        ),
        name="near_late" if late else "near_early",
    )(masks, *arrays)


def far_kernel(late, masks, state, spot, near_acc, left, right, r0, r1, places, tiles, acc):
    spans, weights = [], []
    for t, both in enumerate((left, right)):
        spread_places(both[OBS_ROWS : OBS_ROWS + PAD, :EDGE], places, t * SPAN)
        spans.append(((len(TURNS) - 1) * SPAN_KEYS + t * RANGE_BLOCKS, t * SPAN, both))
        weights.append(both.at[OBS_ROWS + PAD :])
    _, x = own_place(late)
    parity = lax.shift_right_logical(x, 1)
    segments = [(spans, weights)]
    tile_pass(segments, parity, state, spot, acc, places, tiles, masks, near_acc)
    for k, out in enumerate((r0, r1)):
        half = jnp.bitwise_and(jnp.bitwise_xor(x, k), 1)
        start = pl.multiple_of(half * SHARD, SHARD)
        for z in range(NZ):
            out[z * SHARD : (z + 1) * SHARD] = acc[z, pl.ds(start, SHARD), :].astype(out.dtype)


def far(late, masks, state, spot, acc, arrays):
    rows = NZ * SHARD
    return pl.pallas_call(
        functools.partial(far_kernel, late),
        out_shape=(
            jax.ShapeDtypeStruct((rows, MEMBERS), jnp.bfloat16 if late else jnp.float32),
            jax.ShapeDtypeStruct((rows, MEMBERS), jnp.bfloat16),
        ),
        in_specs=[VMEM] * 6,
        out_specs=(VMEM, VMEM),
        scratch_shapes=SCRATCH + [pltpu.VMEM((NZ, EDGE, MEMBERS), jnp.float32)],
        compiler_params=pltpu.CompilerParams(vmem_limit_bytes=20 << 20),
        cost_estimate=pl.CostEstimate(
            flops=500_000_000, transcendentals=500_000, bytes_accessed=4_000_000
        ),
        name="far_late" if late else "far_early",
    )(masks, state, spot, acc, *arrays)


def sum_x_kernel(own, x1, x2, x3, keep, z2, z4, z6):
    my_z = lax.shift_right_logical(lax.axis_index("obs"), 2)
    for mask in range(NZ):
        rows = pl.ds(pl.multiple_of(jnp.bitwise_xor(my_z, mask) * SHARD, SHARD), SHARD)
        total = own[rows, :]
        for ref in (x1, x2, x3):
            total += ref[rows, :].astype(jnp.float32)
        out, k = (keep, z2, z4, z6)[mask // 2], mask & 1
        out[k * SHARD : (k + 1) * SHARD] = total.astype(out.dtype)


def sum_z_kernel(keep, z2, z4, z6, own, send):
    for k, out in enumerate((own, send)):
        rows = slice(k * SHARD, (k + 1) * SHARD)
        total = keep[rows]
        for ref in (z2, z4, z6):
            total += ref[rows].astype(jnp.float32)
        out[...] = total.astype(out.dtype)


def sum_pair_kernel(own, other, out):
    out[...] = own[...] + other[...].astype(jnp.float32)


def small(body, out_rows, *arrays):
    return pl.pallas_call(
        body,
        out_shape=tuple(
            jax.ShapeDtypeStruct((rows, MEMBERS), jnp.bfloat16 if n else jnp.float32)
            for n, rows in enumerate(out_rows)
        ),
        in_specs=[VMEM] * len(arrays),
        out_specs=(VMEM,) * len(out_rows),
        compiler_params=pltpu.CompilerParams(vmem_limit_bytes=6 << 20),
    )(*arrays)


def pack_kernel(*refs):
    out = refs[-1]
    held = (refs[0].shape[0] - PAD) // SHARD
    places = []
    for q, ref in enumerate(refs[:-1]):
        for i in range(held):
            p = q * held + i
            out[p * SHARD : (p + 1) * SHARD] = ref[i * SHARD : (i + 1) * SHARD]
        places.append(ref[held * SHARD :].astype(jnp.float32)[:held])
    count = held * (len(refs) - 1)
    places.append(jnp.zeros((PAD - count, MEMBERS), jnp.float32))
    out[count * SHARD :] = jnp.concatenate(places, axis=0).astype(jnp.bfloat16)


def pack(*parts):
    count = len(parts) * (parts[0].shape[0] - PAD) // SHARD
    return pl.pallas_call(
        pack_kernel,
        out_shape=jax.ShapeDtypeStruct((count * SHARD + PAD, MEMBERS), jnp.bfloat16),
        in_specs=[VMEM] * len(parts),
        out_specs=VMEM,
        compiler_params=pltpu.CompilerParams(vmem_limit_bytes=4 << 20),
        name="pack",
    )(*parts)


def load_kernel(
    state_in, state_pos, obs_in, obs_pos, state, obs, state_places, obs_places, sems
):
    copies = [
        pltpu.make_async_copy(state_pos, state_places, sems.at[0]),
        pltpu.make_async_copy(state_in.at[0], state.at[:SHARD], sems.at[1]),
        pltpu.make_async_copy(obs_pos, obs_places, sems.at[2]),
        pltpu.make_async_copy(obs_in.at[0, 0], obs.at[0, :OBS_ROWS], sems.at[3]),
        pltpu.make_async_copy(obs_in.at[1, 0], obs.at[1, :OBS_ROWS], sems.at[4]),
    ]
    for copy in copies:
        copy.start()
    copies[0].wait()
    held = state_places[...].astype(jnp.float32)
    row = jnp.concatenate([held, jnp.zeros((1, MEMBERS - SHARD), jnp.float32)], axis=1)
    rows = jnp.concatenate([row, jnp.zeros((PAD - 1, MEMBERS), jnp.float32)], axis=0)
    state[SHARD:] = rows.astype(jnp.bfloat16)
    copies[2].wait()
    for t in range(BATCHES):
        held = obs_places[t : t + 1].astype(jnp.float32)
        rows = [held[:, r * EDGE : (r + 1) * EDGE] for r in range(SPAN)]
        rows.append(jnp.zeros((PAD - SPAN, EDGE), jnp.float32))
        obs[t, OBS_ROWS:, :EDGE] = jnp.concatenate(rows, axis=0).astype(jnp.bfloat16)
        obs[t, OBS_ROWS:, EDGE:] = jnp.zeros((PAD, MEMBERS - EDGE), jnp.bfloat16)
    for k in (1, 3, 4):
        copies[k].wait()


def load(state, state_pos, obs, obs_pos):
    return pl.pallas_call(
        load_kernel,
        out_shape=(
            jax.ShapeDtypeStruct((SHARD + PAD, MEMBERS), jnp.bfloat16),
            jax.ShapeDtypeStruct((BATCHES, OBS_ROWS + PAD, MEMBERS), jnp.bfloat16),
        ),
        in_specs=[pl.BlockSpec(memory_space=pltpu.HBM)] * 4,
        out_specs=(VMEM, VMEM),
        scratch_shapes=[
            pltpu.VMEM((1, SHARD), jnp.bfloat16),
            pltpu.VMEM((BATCHES, SPAN * EDGE), jnp.bfloat16),
            pltpu.SemaphoreType.DMA((5,)),
        ],
        compiler_params=pltpu.CompilerParams(vmem_limit_bytes=8 << 20),
        name="load",
    )(state, state_pos, obs, obs_pos)


def relay_kernel(batch, obs, weights, out):
    out[: OBS_ROWS + PAD] = obs[batch]
    out[OBS_ROWS + PAD :] = weights[batch]


def relay(batch, obs, weights):
    return pl.pallas_call(
        functools.partial(relay_kernel, batch),
        out_shape=jax.ShapeDtypeStruct((2 * OBS_ROWS + PAD, MEMBERS), jnp.bfloat16),
        in_specs=[VMEM, VMEM],
        out_specs=VMEM,
        compiler_params=pltpu.CompilerParams(vmem_limit_bytes=8 << 20),
        name="relay",
    )(obs, weights)


def local(ens_state, state_pos, obs_ens, obs_pos, innov_weight, block_rows):
    state, obs = load(ens_state, state_pos[None], obs_ens, obs_pos)
    mine = flip(state)
    other = swap_z_flip(state, 1)
    state = pack(mine, other)
    parts = [state]
    for mask in (4, 2, 6):
        parts.append(swap_z(state, mask))
    state = pack(*parts)
    pieces = [state]
    for k in range(1, NX):
        pieces.append(swap_x(state, k))

    weight = innov_weight[:, 0]
    weight_left = along_rows(weight, 1)
    weight_right = along_rows(weight, ROWS - 1)
    obs_left = along_rows_flip(obs, 1)
    obs_right = along_rows_flip(obs, ROWS - 1)
    obs_own = flip(obs)
    far0 = relay(0, obs_left, weight_left)
    far0 = along_rows(far0, 1)
    far1 = relay(1, obs_right, weight_right)
    far1 = along_rows(far1, ROWS - 1)

    masks = make_masks(jnp.transpose(block_rows, (0, 2, 1)))
    seen = (obs_own, weight, obs_left, weight_left, obs_right, weight_right)
    early = near(0, masks, (pieces[0], pieces[1], *seen))
    later = near(1, masks, (pieces[2], pieces[3], *seen))
    part2, part3 = far(1, masks, *later, (far0, far1))
    part2 = swap_x(part2, 2)
    part3 = swap_x(part3, 3)
    own, part1 = far(0, masks, *early, (far0, far1))
    part1 = swap_x(part1, 1)
    parts = [part1, part2, part3]
    keep, *parts = small(sum_x_kernel, (2 * SHARD,) * 4, own, *parts)
    for k, mask in ((1, 4), (0, 2), (2, 6)):
        parts[k] = swap_z(parts[k], mask)
    own, other = small(sum_z_kernel, (SHARD, SHARD), keep, *parts)
    other = swap_z(other, 1)
    (total,) = small(sum_pair_kernel, (SHARD,), own, other)
    return total[None]


def solution(mesh):
    in_specs = (
        P("half", ("rows", "obs"), None),
        P(("rows", "obs")),
        P(None, "half", ("rows", "obs"), None),
        P(None, ("rows", "obs")),
        P(None, "half", ("rows", "obs"), None),
        P(),
    )
    out_specs = P("half", ("rows", "obs"), None)
    return jax.shard_map(local, mesh=mesh, in_specs=in_specs, out_specs=out_specs, check_vma=False)
```

```python
import functools
import math

import jax
import jax.numpy as jnp
from jax import lax
from jax.experimental import pallas as pl
from jax.experimental.pallas import tpu as pltpu
from jax.sharding import PartitionSpec as P


BATCHES = 2
ROWS, HALVES, OBS = 4, 2, 32
NX, NZ = 4, 8
EDGE = 128
SHARD = 64
MEMBERS = 256
RANGE_BLOCKS = 16
SPAN = 4
NAMED = 16
OBS_ROWS = SPAN * EDGE
PAD = 16
Z_ORDER = (0, 1, 4, 5, 2, 3, 6, 7)

TURNS = (0, ROWS - 1, 1, 2)
SPAN_KEYS = BATCHES * RANGE_BLOCKS
DEAD = -1e30
LIVE = math.log2(1.0 / (MEMBERS - 1))
STRETCH = 2.0 * math.sqrt(math.log2(math.e))

VMEM = pl.BlockSpec(memory_space=pltpu.VMEM)


def flip(value):
    return lax.ppermute(value, "half", [(0, 1), (1, 0)])


def along_rows(value, step):
    return lax.ppermute(value, "rows", [(s, (s + step) % ROWS) for s in range(ROWS)])


def along_rows_flip(value, step):
    pairs = [
        (r * HALVES + h, ((r + step) % ROWS) * HALVES + 1 - h)
        for r in range(ROWS)
        for h in range(HALVES)
    ]
    return lax.ppermute(value, ("rows", "half"), pairs)


def swap_z(value, mask):
    pairs = [(z * NX + x, (z ^ mask) * NX + x) for z in range(NZ) for x in range(NX)]
    return lax.ppermute(value, "obs", pairs)


def swap_z_flip(value, mask):
    pairs = [
        (h * OBS + z * NX + x, (1 - h) * OBS + (z ^ mask) * NX + x)
        for h in range(HALVES)
        for z in range(NZ)
        for x in range(NX)
    ]
    return lax.ppermute(value, ("half", "obs"), pairs)


def swap_x(value, mask):
    pairs = [(z * NX + x, z * NX + (x ^ mask)) for z in range(NZ) for x in range(NX)]
    return lax.ppermute(value, "obs", pairs)


def masks_kernel(named, masks, hits):
    row, column = lax.axis_index("rows"), lax.axis_index("obs")
    blocks = lax.broadcasted_iota(jnp.int32, (RANGE_BLOCKS, EDGE), 0) + row * RANGE_BLOCKS
    for chunk in range(ROWS):
        for t in range(BATCHES):
            hit = jnp.zeros((RANGE_BLOCKS, EDGE), jnp.float32)
            for e in range(NAMED):
                picked = named[t, e : e + 1, chunk * EDGE : (chunk + 1) * EDGE]
                hit = jnp.where(picked == blocks, 1.0, hit)
            hits[chunk, t * RANGE_BLOCKS : (t + 1) * RANGE_BLOCKS] = hit
    shift = jnp.bitwise_and(EDGE - column * SPAN, EDGE - 1)
    for k, turn in enumerate(TURNS):
        chunk = hits[jnp.bitwise_and(row + turn, ROWS - 1)]
        rolled = pltpu.roll(chunk, shift, 1)
        for j in range(SPAN):
            wide = jnp.broadcast_to(rolled[:, j : j + 1], (SPAN_KEYS, EDGE))
            masks[k * SPAN_KEYS : (k + 1) * SPAN_KEYS, j * EDGE : (j + 1) * EDGE] = jnp.where(
                wide > 0.5, LIVE, DEAD
            )


def make_masks(named):
    return pl.pallas_call(
        masks_kernel,
        out_shape=jax.ShapeDtypeStruct((len(TURNS) * SPAN_KEYS, SPAN * EDGE), jnp.float32),
        in_specs=[VMEM],
        out_specs=VMEM,
        scratch_shapes=[pltpu.VMEM((ROWS, SPAN_KEYS, EDGE), jnp.float32)],
        compiler_params=pltpu.CompilerParams(vmem_limit_bytes=4 << 20),
        cost_estimate=pl.CostEstimate(flops=4_000_000, transcendentals=0, bytes_accessed=4_000_000),
        name="masks",
    )(named)


def tile_pass(segments, mask, piece, spot, places, tiles, masks, base, out):
    column = lax.axis_index("obs")
    my_z = lax.shift_right_logical(column, 2)
    x = jnp.bitwise_xor(jnp.bitwise_and(column, NX - 1), mask)
    parity = lax.shift_right_logical(x, 1)
    blocks = [2 * jnp.bitwise_xor(my_z, z) + parity for z in Z_ORDER]
    rows = NZ * SHARD
    pair = 2 * EDGE

    def make(spans, buffer):
        for u, (key, place, obs) in enumerate(spans):
            for h in range(SPAN // 2):
                here = obs[h * pair : (h + 1) * pair, :]
                products = lax.dot_general(
                    piece[:rows, :], here, (((1,), (1,)), ((), ())),
                    preferred_element_type=jnp.float32,
                )
                for p, block in enumerate(blocks):
                    part_rows = slice(p * SHARD, (p + 1) * SHARD)
                    positions = spot[part_rows]
                    live = masks[pl.ds(key + block, 1), h * pair : (h + 1) * pair]
                    for i in range(2):
                        j = 2 * h + i
                        lanes = slice(i * EDGE, (i + 1) * EDGE)
                        d = positions - places[place + j : place + j + 1, :]
                        damped = products[part_rows, lanes] * jnp.exp2(live[:, lanes] - d * d)
                        at = (u * SPAN + j) * EDGE
                        tiles[buffer, part_rows, at : at + EDGE] = damped.astype(jnp.bfloat16)

    def add(weights, buffer, first):
        start = 0
        total = None
        for weight in weights:
            depth = weight.shape[0]
            part = jnp.dot(
                tiles[buffer, :, start : start + depth], weight[...],
                preferred_element_type=jnp.float32,
            )
            total = part if total is None else total + part
            start += depth
        if not first:
            total = out[...] + total
        elif base is not None:
            total = base[...] + total
        out[...] = total.astype(out.dtype)

    for n, (spans, weights) in enumerate(segments):
        if n:
            add(segments[n - 1][1], (n - 1) % 2, n == 1)
        make(spans, n % 2)
    last = len(segments) - 1
    add(segments[last][1], last % 2, last == 0)


def spread_places(held, places, start):
    places[start : start + SPAN] = held.astype(jnp.float32)[:SPAN] * STRETCH


def near_kernel(mask, masks, piece, oo, wo, ol, wl, orr, wr, spot, acc, places, tiles):
    lanes = lax.broadcasted_iota(jnp.int32, (SHARD, EDGE), 1)
    sublanes = lax.broadcasted_iota(jnp.int32, (SHARD, EDGE), 0)
    same = lanes == sublanes
    ones = jnp.ones((EDGE, EDGE), jnp.bfloat16)
    held = piece[NZ * SHARD : NZ * SHARD + PAD, :EDGE].astype(jnp.float32)
    spread = jnp.concatenate(
        [jnp.where(same, held[p : p + 1], 0.0) for p in range(NZ)], axis=0
    ).astype(jnp.bfloat16)
    spot[...] = jnp.dot(spread, ones, preferred_element_type=jnp.float32) * STRETCH
    segments = []
    for k, (o, w) in enumerate(((oo, wo), (ol, wl), (orr, wr))):
        spans = []
        for t in range(BATCHES):
            place = (k * BATCHES + t) * SPAN
            spread_places(o[t, OBS_ROWS : OBS_ROWS + PAD, :EDGE], places, place)
            spans.append((k * SPAN_KEYS + t * RANGE_BLOCKS, place, o.at[t]))
        segments.append((spans, (w.reshape(BATCHES * OBS_ROWS, MEMBERS),)))
    tile_pass(segments, mask, piece, spot, places, tiles, masks, None, acc)


SCRATCH = [
    pltpu.VMEM((24, EDGE), jnp.float32),
    pltpu.VMEM((2, NZ * SHARD, BATCHES * SPAN * EDGE), jnp.bfloat16),
]


def near(mask, masks, arrays):
    return pl.pallas_call(
        functools.partial(near_kernel, mask),
        out_shape=(
            jax.ShapeDtypeStruct((NZ * SHARD, EDGE), jnp.float32),
            jax.ShapeDtypeStruct((NZ * SHARD, MEMBERS), jnp.float32),
        ),
        in_specs=[VMEM] * 8,
        out_specs=(VMEM,) * 2,
        scratch_shapes=SCRATCH,
        compiler_params=pltpu.CompilerParams(vmem_limit_bytes=16 << 20),
        cost_estimate=pl.CostEstimate(
            flops=1_000_000_000, transcendentals=1_000_000, bytes_accessed=4_000_000
        ),
    )(masks, *arrays)


def far_kernel(mask, masks, piece, spot, acc, left, right, out, places, tiles):
    spans, weights = [], []
    for t, both in enumerate((left, right)):
        spread_places(both[OBS_ROWS : OBS_ROWS + PAD, :EDGE], places, t * SPAN)
        spans.append(((len(TURNS) - 1) * SPAN_KEYS + t * RANGE_BLOCKS, t * SPAN, both))
        weights.append(both.at[OBS_ROWS + PAD :])
    tile_pass([(spans, weights)], mask, piece, spot, places, tiles, masks, acc, out)


def far(mask, masks, piece, spot, acc, arrays):
    return pl.pallas_call(
        functools.partial(far_kernel, mask),
        out_shape=jax.ShapeDtypeStruct(
            (NZ * SHARD, MEMBERS), jnp.bfloat16 if mask else jnp.float32
        ),
        in_specs=[VMEM] * 6,
        out_specs=VMEM,
        scratch_shapes=SCRATCH,
        compiler_params=pltpu.CompilerParams(vmem_limit_bytes=16 << 20),
        cost_estimate=pl.CostEstimate(
            flops=300_000_000, transcendentals=300_000, bytes_accessed=4_000_000
        ),
    )(masks, piece, spot, acc, *arrays)


def sum_x_kernel(own, x1, x2, x3, keep, send):
    for p in range(NZ):
        rows = slice(p * SHARD, (p + 1) * SHARD)
        total = own[rows]
        for ref in (x1, x2, x3):
            total += ref[rows].astype(jnp.float32)
        out, k = (keep, send)[p & 1], p // 2
        out[k * SHARD : (k + 1) * SHARD] = total.astype(out.dtype)


def sum_pair_kernel(keep, got, own, z4, z2, z6):
    for k, out in enumerate((own, z4, z2, z6)):
        rows = slice(k * SHARD, (k + 1) * SHARD)
        out[...] = (keep[rows] + got[rows].astype(jnp.float32)).astype(out.dtype)


def sum_z_kernel(own, z4, z2, z6, out):
    total = own[...]
    for ref in (z4, z2, z6):
        total += ref[...].astype(jnp.float32)
    out[...] = total


def small(body, out_rows, *arrays):
    return pl.pallas_call(
        body,
        out_shape=tuple(
            jax.ShapeDtypeStruct((rows, MEMBERS), jnp.bfloat16 if n else jnp.float32)
            for n, rows in enumerate(out_rows)
        ),
        in_specs=[VMEM] * len(arrays),
        out_specs=(VMEM,) * len(out_rows),
        compiler_params=pltpu.CompilerParams(vmem_limit_bytes=6 << 20),
    )(*arrays)


def pack_kernel(*refs):
    out = refs[-1]
    held = (refs[0].shape[0] - PAD) // SHARD
    places = []
    for q, ref in enumerate(refs[:-1]):
        for i in range(held):
            p = q * held + i
            out[p * SHARD : (p + 1) * SHARD] = ref[i * SHARD : (i + 1) * SHARD]
        places.append(ref[held * SHARD :].astype(jnp.float32)[:held])
    count = held * (len(refs) - 1)
    places.append(jnp.zeros((PAD - count, MEMBERS), jnp.float32))
    out[count * SHARD :] = jnp.concatenate(places, axis=0).astype(jnp.bfloat16)


def pack(*parts):
    count = len(parts) * (parts[0].shape[0] - PAD) // SHARD
    return pl.pallas_call(
        pack_kernel,
        out_shape=jax.ShapeDtypeStruct((count * SHARD + PAD, MEMBERS), jnp.bfloat16),
        in_specs=[VMEM] * len(parts),
        out_specs=VMEM,
        compiler_params=pltpu.CompilerParams(vmem_limit_bytes=4 << 20),
        name="pack",
    )(*parts)


def load_kernel(
    state_in, state_pos, obs_in, obs_pos, state, obs, state_places, obs_places, sems
):
    copies = [
        pltpu.make_async_copy(state_pos, state_places, sems.at[0]),
        pltpu.make_async_copy(state_in.at[0], state.at[:SHARD], sems.at[1]),
        pltpu.make_async_copy(obs_pos, obs_places, sems.at[2]),
        pltpu.make_async_copy(obs_in.at[0, 0], obs.at[0, :OBS_ROWS], sems.at[3]),
        pltpu.make_async_copy(obs_in.at[1, 0], obs.at[1, :OBS_ROWS], sems.at[4]),
    ]
    for copy in copies:
        copy.start()
    copies[0].wait()
    held = state_places[...].astype(jnp.float32)
    row = jnp.concatenate([held, jnp.zeros((1, MEMBERS - SHARD), jnp.float32)], axis=1)
    rows = jnp.concatenate([row, jnp.zeros((PAD - 1, MEMBERS), jnp.float32)], axis=0)
    state[SHARD:] = rows.astype(jnp.bfloat16)
    copies[2].wait()
    for t in range(BATCHES):
        held = obs_places[t : t + 1].astype(jnp.float32)
        rows = [held[:, r * EDGE : (r + 1) * EDGE] for r in range(SPAN)]
        rows.append(jnp.zeros((PAD - SPAN, EDGE), jnp.float32))
        obs[t, OBS_ROWS:, :EDGE] = jnp.concatenate(rows, axis=0).astype(jnp.bfloat16)
        obs[t, OBS_ROWS:, EDGE:] = jnp.zeros((PAD, MEMBERS - EDGE), jnp.bfloat16)
    for k in (1, 3, 4):
        copies[k].wait()


def load(state, state_pos, obs, obs_pos):
    return pl.pallas_call(
        load_kernel,
        out_shape=(
            jax.ShapeDtypeStruct((SHARD + PAD, MEMBERS), jnp.bfloat16),
            jax.ShapeDtypeStruct((BATCHES, OBS_ROWS + PAD, MEMBERS), jnp.bfloat16),
        ),
        in_specs=[pl.BlockSpec(memory_space=pltpu.HBM)] * 4,
        out_specs=(VMEM, VMEM),
        scratch_shapes=[
            pltpu.VMEM((1, SHARD), jnp.bfloat16),
            pltpu.VMEM((BATCHES, SPAN * EDGE), jnp.bfloat16),
            pltpu.SemaphoreType.DMA((5,)),
        ],
        compiler_params=pltpu.CompilerParams(vmem_limit_bytes=8 << 20),
        name="load",
    )(state, state_pos, obs, obs_pos)


def relay_kernel(batch, obs, weights, out):
    out[: OBS_ROWS + PAD] = obs[batch]
    out[OBS_ROWS + PAD :] = weights[batch]


def relay(batch, obs, weights):
    return pl.pallas_call(
        functools.partial(relay_kernel, batch),
        out_shape=jax.ShapeDtypeStruct((2 * OBS_ROWS + PAD, MEMBERS), jnp.bfloat16),
        in_specs=[VMEM, VMEM],
        out_specs=VMEM,
        compiler_params=pltpu.CompilerParams(vmem_limit_bytes=8 << 20),
        name="relay",
    )(obs, weights)


def local(ens_state, state_pos, obs_ens, obs_pos, innov_weight, block_rows):
    given = (ens_state, state_pos[None], obs_ens, obs_pos)
    state, obs = load(*(pltpu.with_memory_space_constraint(v, pltpu.HBM) for v in given))
    mine = flip(state)
    other = swap_z_flip(state, 1)
    state = pack(mine, other)
    parts = [state]
    for mask in (4, 2, 6):
        parts.append(swap_z(state, mask))
    state = pack(*parts)
    pieces = [state]
    for k in range(1, NX):
        pieces.append(swap_x(state, k))

    weight = innov_weight[:, 0]
    weight_left = along_rows(weight, 1)
    weight_right = along_rows(weight, ROWS - 1)
    obs_left = along_rows_flip(obs, 1)
    obs_right = along_rows_flip(obs, ROWS - 1)
    obs_own = flip(obs)
    far0 = relay(0, obs_left, weight_left)
    far0 = along_rows(far0, 1)
    far1 = relay(1, obs_right, weight_right)
    far1 = along_rows(far1, ROWS - 1)

    masks = make_masks(jnp.transpose(block_rows, (0, 2, 1)))
    seen = (obs_own, weight, obs_left, weight_left, obs_right, weight_right)
    held = []
    for mask in range(NX):
        held.append(near(mask, masks, (pieces[mask], *seen)))
    parts = [None] * NX
    for mask in (2, 3, 1, 0):
        parts[mask] = far(mask, masks, pieces[mask], *held[mask], (far0, far1))
        if mask:
            parts[mask] = swap_x(parts[mask], mask)
    keep, send = small(sum_x_kernel, (4 * SHARD,) * 2, *parts)
    got = swap_z(send, 1)
    own, *parts = small(sum_pair_kernel, (SHARD,) * 4, keep, got)
    for k, mask in enumerate((4, 2, 6)):
        parts[k] = swap_z(parts[k], mask)
    (total,) = small(sum_z_kernel, (SHARD,), own, *parts)
    return total[None]


def solution(mesh):
    in_specs = (
        P("half", ("rows", "obs"), None),
        P(("rows", "obs")),
        P(None, "half", ("rows", "obs"), None),
        P(None, ("rows", "obs")),
        P(None, "half", ("rows", "obs"), None),
        P(),
    )
    out_specs = P("half", ("rows", "obs"), None)
    return jax.shard_map(local, mesh=mesh, in_specs=in_specs, out_specs=out_specs, check_vma=False)
```

```python
import functools
import math

import jax
import jax.numpy as jnp
from jax import lax
from jax.experimental import pallas as pl
from jax.experimental.pallas import tpu as pltpu
from jax.sharding import PartitionSpec as P


BATCHES = 2
ROWS, HALVES, OBS = 4, 2, 32
NX, NZ = 4, 8
EDGE = 128
SHARD = 64
MEMBERS = 256
RANGE_BLOCKS = 16
SPAN = 4
NAMED = 16
OBS_ROWS = SPAN * EDGE
PAD = 16
Z_ORDER = (0, 1, 4, 5, 2, 3, 6, 7)

TURNS = (0, ROWS - 1, 1, 2)
SPAN_KEYS = BATCHES * RANGE_BLOCKS
DEAD = -1e30
LIVE = math.log2(1.0 / (MEMBERS - 1))
STRETCH = 2.0 * math.sqrt(math.log2(math.e))

VMEM = pl.BlockSpec(memory_space=pltpu.VMEM)


def flip(value):
    return lax.ppermute(value, "half", [(0, 1), (1, 0)])


def along_rows(value, step):
    return lax.ppermute(value, "rows", [(s, (s + step) % ROWS) for s in range(ROWS)])


def along_rows_flip(value, step):
    pairs = [
        (r * HALVES + h, ((r + step) % ROWS) * HALVES + 1 - h)
        for r in range(ROWS)
        for h in range(HALVES)
    ]
    return lax.ppermute(value, ("rows", "half"), pairs)


def swap_z(value, mask):
    pairs = [(z * NX + x, (z ^ mask) * NX + x) for z in range(NZ) for x in range(NX)]
    return lax.ppermute(value, "obs", pairs)


def swap_z_flip(value, mask):
    pairs = [
        (h * OBS + z * NX + x, (1 - h) * OBS + (z ^ mask) * NX + x)
        for h in range(HALVES)
        for z in range(NZ)
        for x in range(NX)
    ]
    return lax.ppermute(value, ("half", "obs"), pairs)


def swap_x(value, mask):
    pairs = [(z * NX + x, z * NX + (x ^ mask)) for z in range(NZ) for x in range(NX)]
    return lax.ppermute(value, "obs", pairs)


def masks_kernel(named, masks, hits):
    row, column = lax.axis_index("rows"), lax.axis_index("obs")
    blocks = lax.broadcasted_iota(jnp.int32, (RANGE_BLOCKS, EDGE), 0) + row * RANGE_BLOCKS
    for chunk in range(ROWS):
        for t in range(BATCHES):
            hit = jnp.zeros((RANGE_BLOCKS, EDGE), jnp.float32)
            for e in range(NAMED):
                picked = named[t, e : e + 1, chunk * EDGE : (chunk + 1) * EDGE]
                hit = jnp.where(picked == blocks, 1.0, hit)
            hits[chunk, t * RANGE_BLOCKS : (t + 1) * RANGE_BLOCKS] = hit
    shift = jnp.bitwise_and(EDGE - column * SPAN, EDGE - 1)
    for k, turn in enumerate(TURNS):
        chunk = hits[jnp.bitwise_and(row + turn, ROWS - 1)]
        rolled = pltpu.roll(chunk, shift, 1)
        for j in range(SPAN):
            wide = jnp.broadcast_to(rolled[:, j : j + 1], (SPAN_KEYS, EDGE))
            masks[k * SPAN_KEYS : (k + 1) * SPAN_KEYS, j * EDGE : (j + 1) * EDGE] = jnp.where(
                wide > 0.5, LIVE, DEAD
            )


def make_masks(named):
    return pl.pallas_call(
        masks_kernel,
        out_shape=jax.ShapeDtypeStruct((len(TURNS) * SPAN_KEYS, SPAN * EDGE), jnp.float32),
        in_specs=[VMEM],
        out_specs=VMEM,
        scratch_shapes=[pltpu.VMEM((ROWS, SPAN_KEYS, EDGE), jnp.float32)],
        compiler_params=pltpu.CompilerParams(vmem_limit_bytes=4 << 20),
        cost_estimate=pl.CostEstimate(flops=4_000_000, transcendentals=0, bytes_accessed=4_000_000),
        name="masks",
    )(named)


def tile_pass(segments, mask, piece, spot, places, tiles, masks, base, held, out):
    column = lax.axis_index("obs")
    my_z = lax.shift_right_logical(column, 2)
    x = jnp.bitwise_xor(jnp.bitwise_and(column, NX - 1), mask)
    parity = lax.shift_right_logical(x, 1)
    blocks = [2 * jnp.bitwise_xor(my_z, z) + parity for z in Z_ORDER]
    rows = NZ * SHARD
    pair = 2 * EDGE

    def make(spans, buffer):
        for u, (key, place, obs) in enumerate(spans):
            for h in range(SPAN // 2):
                here = obs[h * pair : (h + 1) * pair, :]
                products = lax.dot_general(
                    piece[:rows, :], here, (((1,), (1,)), ((), ())),
                    preferred_element_type=jnp.float32,
                )
                for p, block in enumerate(blocks):
                    part_rows = slice(p * SHARD, (p + 1) * SHARD)
                    positions = spot[part_rows]
                    live = masks[pl.ds(key + block, 1), h * pair : (h + 1) * pair]
                    for i in range(2):
                        j = 2 * h + i
                        lanes = slice(i * EDGE, (i + 1) * EDGE)
                        d = positions - places[place + j : place + j + 1, :]
                        damped = products[part_rows, lanes] * jnp.exp2(live[:, lanes] - d * d)
                        at = (u * SPAN + j) * EDGE
                        tiles[buffer, part_rows, at : at + EDGE] = damped.astype(jnp.bfloat16)

    def add(weight, buffer, first, out):
        depth = weight.shape[0]
        total = jnp.dot(
            tiles[buffer, :, :depth], weight[...], preferred_element_type=jnp.float32
        )
        if not first:
            total = held[...] + total
        elif base is not None:
            total = base[...] + total
        out[...] = total.astype(out.dtype)

    for n, (spans, weight) in enumerate(segments):
        if n:
            add(segments[n - 1][1], (n - 1) % 2, n == 1, held)
        make(spans, n % 2)
    last = len(segments) - 1
    add(segments[last][1], last % 2, last == 0, out)


def spread_places(held, places, start):
    places[start : start + SPAN] = held.astype(jnp.float32)[:SPAN] * STRETCH


def near_kernel(mask, masks, piece, oo, wo, ol, wl, orr, wr, spot, acc, places, tiles):
    lanes = lax.broadcasted_iota(jnp.int32, (SHARD, EDGE), 1)
    sublanes = lax.broadcasted_iota(jnp.int32, (SHARD, EDGE), 0)
    same = lanes == sublanes
    ones = jnp.ones((EDGE, EDGE), jnp.bfloat16)
    held = piece[NZ * SHARD : NZ * SHARD + PAD, :EDGE].astype(jnp.float32)
    spread = jnp.concatenate(
        [jnp.where(same, held[p : p + 1], 0.0) for p in range(NZ)], axis=0
    ).astype(jnp.bfloat16)
    spot[...] = jnp.dot(spread, ones, preferred_element_type=jnp.float32) * STRETCH
    segments = []
    for k, (o, w) in enumerate(((oo, wo), (ol, wl), (orr, wr))):
        spans = []
        for t in range(BATCHES):
            place = (k * BATCHES + t) * SPAN
            spread_places(o[t, OBS_ROWS : OBS_ROWS + PAD, :EDGE], places, place)
            spans.append((k * SPAN_KEYS + t * RANGE_BLOCKS, place, o.at[t]))
        segments.append((spans, w.reshape(BATCHES * OBS_ROWS, MEMBERS)))
    tile_pass(segments, mask, piece, spot, places, tiles, masks, None, acc, acc)


SCRATCH = [
    pltpu.VMEM((24, EDGE), jnp.float32),
    pltpu.VMEM((2, NZ * SHARD, BATCHES * SPAN * EDGE), jnp.bfloat16),
]


def near(mask, masks, arrays):
    return pl.pallas_call(
        functools.partial(near_kernel, mask),
        out_shape=(
            jax.ShapeDtypeStruct((NZ * SHARD, EDGE), jnp.float32),
            jax.ShapeDtypeStruct((NZ * SHARD, MEMBERS), jnp.float32),
        ),
        in_specs=[VMEM] * 8,
        out_specs=(VMEM,) * 2,
        scratch_shapes=SCRATCH,
        compiler_params=pltpu.CompilerParams(vmem_limit_bytes=16 << 20),
        cost_estimate=pl.CostEstimate(
            flops=1_000_000_000, transcendentals=1_000_000, bytes_accessed=4_000_000
        ),
    )(masks, *arrays)


def far_kernel(mask, masks, piece, spot, acc, left, right, out, places, tiles, held):
    segments = []
    for t, both in enumerate((left, right)):
        spread_places(both[OBS_ROWS : OBS_ROWS + PAD, :EDGE], places, t * SPAN)
        span = ((len(TURNS) - 1) * SPAN_KEYS + t * RANGE_BLOCKS, t * SPAN, both)
        segments.append(([span], both.at[OBS_ROWS + PAD :]))
    tile_pass(segments, mask, piece, spot, places, tiles, masks, acc, held, out)


def far(mask, masks, piece, spot, acc, arrays):
    return pl.pallas_call(
        functools.partial(far_kernel, mask),
        out_shape=jax.ShapeDtypeStruct(
            (NZ * SHARD, MEMBERS), jnp.bfloat16 if mask else jnp.float32
        ),
        in_specs=[VMEM] * 6,
        out_specs=VMEM,
        scratch_shapes=SCRATCH + [pltpu.VMEM((NZ * SHARD, MEMBERS), jnp.float32)],
        compiler_params=pltpu.CompilerParams(vmem_limit_bytes=16 << 20),
        cost_estimate=pl.CostEstimate(
            flops=300_000_000, transcendentals=300_000, bytes_accessed=4_000_000
        ),
    )(masks, piece, spot, acc, *arrays)


def sum_x_kernel(own, x1, x2, x3, keep, send):
    for p in range(NZ):
        rows = slice(p * SHARD, (p + 1) * SHARD)
        total = own[rows]
        for ref in (x1, x2, x3):
            total += ref[rows].astype(jnp.float32)
        out, k = (keep, send)[p & 1], p // 2
        out[k * SHARD : (k + 1) * SHARD] = total.astype(out.dtype)


def sum_pair_kernel(keep, got, own, z4, z2, z6):
    for k, out in enumerate((own, z4, z2, z6)):
        rows = slice(k * SHARD, (k + 1) * SHARD)
        out[...] = (keep[rows] + got[rows].astype(jnp.float32)).astype(out.dtype)


def sum_z_kernel(own, z4, z2, z6, out):
    total = own[...]
    for ref in (z4, z2, z6):
        total += ref[...].astype(jnp.float32)
    out[...] = total


def small(body, out_rows, *arrays):
    return pl.pallas_call(
        body,
        out_shape=tuple(
            jax.ShapeDtypeStruct((rows, MEMBERS), jnp.bfloat16 if n else jnp.float32)
            for n, rows in enumerate(out_rows)
        ),
        in_specs=[VMEM] * len(arrays),
        out_specs=(VMEM,) * len(out_rows),
        compiler_params=pltpu.CompilerParams(vmem_limit_bytes=6 << 20),
    )(*arrays)


def pack_kernel(*refs):
    out = refs[-1]
    held = (refs[0].shape[0] - PAD) // SHARD
    places = []
    for q, ref in enumerate(refs[:-1]):
        for i in range(held):
            p = q * held + i
            out[p * SHARD : (p + 1) * SHARD] = ref[i * SHARD : (i + 1) * SHARD]
        places.append(ref[held * SHARD :].astype(jnp.float32)[:held])
    count = held * (len(refs) - 1)
    places.append(jnp.zeros((PAD - count, MEMBERS), jnp.float32))
    out[count * SHARD :] = jnp.concatenate(places, axis=0).astype(jnp.bfloat16)


def pack(*parts):
    count = len(parts) * (parts[0].shape[0] - PAD) // SHARD
    return pl.pallas_call(
        pack_kernel,
        out_shape=jax.ShapeDtypeStruct((count * SHARD + PAD, MEMBERS), jnp.bfloat16),
        in_specs=[VMEM] * len(parts),
        out_specs=VMEM,
        compiler_params=pltpu.CompilerParams(vmem_limit_bytes=4 << 20),
        name="pack",
    )(*parts)


def load_kernel(
    state_in, state_pos, obs_in, obs_pos, state, obs, state_places, obs_places, sems
):
    copies = [
        pltpu.make_async_copy(state_pos, state_places, sems.at[0]),
        pltpu.make_async_copy(state_in.at[0], state.at[:SHARD], sems.at[1]),
        pltpu.make_async_copy(obs_pos, obs_places, sems.at[2]),
        pltpu.make_async_copy(obs_in.at[0, 0], obs.at[0, :OBS_ROWS], sems.at[3]),
        pltpu.make_async_copy(obs_in.at[1, 0], obs.at[1, :OBS_ROWS], sems.at[4]),
    ]
    for copy in copies:
        copy.start()
    copies[0].wait()
    held = state_places[...].astype(jnp.float32)
    row = jnp.concatenate([held, jnp.zeros((1, MEMBERS - SHARD), jnp.float32)], axis=1)
    rows = jnp.concatenate([row, jnp.zeros((PAD - 1, MEMBERS), jnp.float32)], axis=0)
    state[SHARD:] = rows.astype(jnp.bfloat16)
    copies[2].wait()
    for t in range(BATCHES):
        held = obs_places[t : t + 1].astype(jnp.float32)
        rows = [held[:, r * EDGE : (r + 1) * EDGE] for r in range(SPAN)]
        rows.append(jnp.zeros((PAD - SPAN, EDGE), jnp.float32))
        obs[t, OBS_ROWS:, :EDGE] = jnp.concatenate(rows, axis=0).astype(jnp.bfloat16)
        obs[t, OBS_ROWS:, EDGE:] = jnp.zeros((PAD, MEMBERS - EDGE), jnp.bfloat16)
    for k in (1, 3, 4):
        copies[k].wait()


def load(state, state_pos, obs, obs_pos):
    return pl.pallas_call(
        load_kernel,
        out_shape=(
            jax.ShapeDtypeStruct((SHARD + PAD, MEMBERS), jnp.bfloat16),
            jax.ShapeDtypeStruct((BATCHES, OBS_ROWS + PAD, MEMBERS), jnp.bfloat16),
        ),
        in_specs=[pl.BlockSpec(memory_space=pltpu.HBM)] * 4,
        out_specs=(VMEM, VMEM),
        scratch_shapes=[
            pltpu.VMEM((1, SHARD), jnp.bfloat16),
            pltpu.VMEM((BATCHES, SPAN * EDGE), jnp.bfloat16),
            pltpu.SemaphoreType.DMA((5,)),
        ],
        compiler_params=pltpu.CompilerParams(vmem_limit_bytes=8 << 20),
        name="load",
    )(state, state_pos, obs, obs_pos)


def relay_kernel(batch, obs, weights, out):
    out[: OBS_ROWS + PAD] = obs[batch]
    out[OBS_ROWS + PAD :] = weights[batch]


def relay(batch, obs, weights):
    return pl.pallas_call(
        functools.partial(relay_kernel, batch),
        out_shape=jax.ShapeDtypeStruct((2 * OBS_ROWS + PAD, MEMBERS), jnp.bfloat16),
        in_specs=[VMEM, VMEM],
        out_specs=VMEM,
        compiler_params=pltpu.CompilerParams(vmem_limit_bytes=8 << 20),
        name="relay",
    )(obs, weights)


def local(ens_state, state_pos, obs_ens, obs_pos, innov_weight, block_rows):
    given = (ens_state, state_pos[None], obs_ens, obs_pos)
    state, obs = load(*(pltpu.with_memory_space_constraint(v, pltpu.HBM) for v in given))
    mine = flip(state)
    other = swap_z_flip(state, 1)
    state = pack(mine, other)
    parts = [state]
    for mask in (4, 2, 6):
        parts.append(swap_z(state, mask))
    state = pack(*parts)
    pieces = [state]
    for k in range(1, NX):
        pieces.append(swap_x(state, k))

    weight = innov_weight[:, 0]
    weight_left = along_rows(weight, 1)
    weight_right = along_rows(weight, ROWS - 1)
    obs_left = along_rows_flip(obs, 1)
    obs_right = along_rows_flip(obs, ROWS - 1)
    obs_own = flip(obs)
    far0 = relay(0, obs_left, weight_left)
    far0 = along_rows(far0, 1)
    far1 = relay(1, obs_right, weight_right)
    far1 = along_rows(far1, ROWS - 1)

    masks = make_masks(jnp.transpose(block_rows, (0, 2, 1)))
    seen = (obs_own, weight, obs_left, weight_left, obs_right, weight_right)
    held = []
    for mask in range(NX):
        held.append(near(mask, masks, (pieces[mask], *seen)))
    parts = [None] * NX
    for mask in (1, 3, 2, 0):
        parts[mask] = far(mask, masks, pieces[mask], *held[mask], (far0, far1))
        if mask:
            parts[mask] = swap_x(parts[mask], mask)
    keep, send = small(sum_x_kernel, (4 * SHARD,) * 2, *parts)
    got = swap_z(send, 1)
    own, *parts = small(sum_pair_kernel, (SHARD,) * 4, keep, got)
    for k, mask in enumerate((4, 2, 6)):
        parts[k] = swap_z(parts[k], mask)
    (total,) = small(sum_z_kernel, (SHARD,), own, *parts)
    return total[None]


def solution(mesh):
    in_specs = (
        P("half", ("rows", "obs"), None),
        P(("rows", "obs")),
        P(None, "half", ("rows", "obs"), None),
        P(None, ("rows", "obs")),
        P(None, "half", ("rows", "obs"), None),
        P(),
    )
    out_specs = P("half", ("rows", "obs"), None)
    return jax.shard_map(local, mesh=mesh, in_specs=in_specs, out_specs=out_specs, check_vma=False)
```
